256 devices in a mesh: section: 2 (over core), req: 128 (over x, y, z).
Axes of the slice: x: 4, y: 4, z: 8, core: 2. Of those that a mesh axis runs over, the one named last changes fastest.
Arguments:
- section_in: bfloat16 [2, 128, 32, 1152], P('section', 'req'), may hold values from -24 to 24
- patch_index: int32 [2, 128], P('section', 'req'), may hold values from 0 to 3
- stale_kv: bfloat16 [2, 128, 128, 2304], P('section', 'req'), may hold values from -400 to 400
- modulation: float32 [2, 128, 6, 1152], P('section', 'req'), may hold values from -4 to 4
- final_mod: float32 [128, 2, 1152], P('req'), may hold values from -4 to 4
- qkv_blocks: bfloat16 [2, 128, 1152, 864], P('section', 'req'), may hold values from -1 to 1, as said below
- out_blocks: bfloat16 [2, 128, 1152, 288], P('section', 'req'), may hold values from -1 to 1, as said below
- up_blocks: bfloat16 [2, 128, 1152, 1152], P('section', 'req'), may hold values from -1 to 1, as said below
- down_blocks: bfloat16 [2, 128, 1152, 1152], P('section', 'req'), may hold values from -1 to 1, as said below
- final_weight: bfloat16 [1152, 16], replicated, may hold values from -0.1875 to 0.1875
- noisy_latent: float32 [128, 512], P('req', 'section'), may hold values from -6 to 6
- time_index: int32 [128], P('req'), may hold values from 100 to 499
- time_gap: int32 [128], P('req'), may hold values from 10 to 40
Outputs:
- fresh_kv: bfloat16 [2, 128, 32, 2304], P('section', 'req')
- next_input: bfloat16 [128, 32, 1152], P('req', 'section')
- noise_pred: float32 [128, 512], P('req', 'section')
- denoised: float32 [128, 512], P('req', 'section')
The draws below stay inside these ranges and needn't reach their ends.
Inputs may be any that keep to these rules, and one draw needn't show every extreme that they name: qkv_blocks[s, r] equals qkv_blocks[s, r mod 4]. out_blocks[s, r] equals out_blocks[s, r mod 4]. up_blocks[s, r] equals up_blocks[s, r mod 4]. down_blocks[s, r] equals down_blocks[s, r mod 4].
All inputs are finite; a program needn't handle non-finite values.
Results may differ from the reference program's by a relative error of at most 0.0093.
Values may be sent and summed in bfloat16 or wider, within the bound.
A program may use at most 64 MiB of HBM per device.

```python
import math
import jax
import jax.numpy as jnp
from jax import lax

D = 1152
HEADS = 16
FF = 4608
CH = 16
PATCHES = 4
UNIT_GROUPS = 4
PATCH_TOK = 32
LAT_TOK = 128
LAYERS = 2
REQS = 128
WEIGHT_COPIES = 128


def clipped_normal(key, extent):
    return jnp.clip(jax.random.normal(key, extent, jnp.float32), -4.0, 4.0)


def tiled_blocks(key, rows_in, columns, fan_in):
    blocks = clipped_normal(key, (LAYERS, UNIT_GROUPS, rows_in, columns)) * fan_in ** (-0.5)
    copies = jnp.arange(WEIGHT_COPIES, dtype=jnp.int32) % UNIT_GROUPS
    return jnp.take(blocks, copies, axis=1).astype(jnp.bfloat16)


def draw_section_in(key, part):
    seeded = jax.random.fold_in(key, 11)
    key_row, key_col, key_main = jax.random.split(seeded, 3)
    extent = (LAYERS, REQS, PATCH_TOK, D)
    row_scale = jnp.exp(jax.random.uniform(key_row, (LAYERS, REQS, PATCH_TOK, 1), jnp.float32, math.log(0.3), math.log(3.0)))
    column_scale = jnp.exp(jax.random.uniform(key_col, (1, 1, 1, D), jnp.float32, math.log(0.5), math.log(2.0)))
    entries = clipped_normal(key_main, extent)
    return (entries * row_scale * column_scale).astype(jnp.bfloat16)


def draw_stale_kv(key, part):
    seeded = jax.random.fold_in(key, 37)
    key_keys, key_values = jax.random.split(seeded, 2)
    key_rows = 2.0 * clipped_normal(key_keys, (LAYERS, REQS, LAT_TOK, D))
    value_rows = 1.5 * clipped_normal(key_values, (LAYERS, REQS, LAT_TOK, D))
    return jnp.concatenate([key_rows, value_rows], axis=-1).astype(jnp.bfloat16)


def draw_qkv_blocks(key, part):
    return tiled_blocks(jax.random.fold_in(key, 41), D, 3 * D // UNIT_GROUPS, D)


def draw_out_blocks(key, part):
    return tiled_blocks(jax.random.fold_in(key, 43), D, D // UNIT_GROUPS, D)


def draw_up_blocks(key, part):
    return tiled_blocks(jax.random.fold_in(key, 47), D, FF // UNIT_GROUPS, D)


def draw_down_blocks(key, part):
    return tiled_blocks(jax.random.fold_in(key, 53), FF // UNIT_GROUPS, D, FF)


def touch_ends(values, rng, low, largest):
    longest = values.shape.index(max(values.shape))
    spots = []
    for shift in (0, 1):
        where = [jax.random.randint(jax.random.fold_in(rng, axis), (), 0, length) for axis, length in enumerate(values.shape)]
        where[longest] = (where[longest] + shift) % values.shape[longest]
        spots.append(tuple(where))
    return values.at[spots[0]].set(low).at[spots[1]].set(largest)


def block_scale(own_key, dims, shards, low, high):
    def one(position, blocks):
        steps = jax.random.uniform(jax.random.fold_in(jax.random.fold_in(own_key, 6), position), (blocks,), jnp.float32, low / len(shards), high / len(shards))
        return jnp.repeat(jnp.exp(steps), dims[position] // blocks).reshape((-1,) + (1,) * (len(dims) - position - 1))

    level = one(*shards[0])
    for cut in shards[1:]:
        level = level * one(*cut)
    return level


def normal_values(own_key, dims, scale, limit, shards=(), held_as=jnp.bfloat16):
    values = jax.random.normal(own_key, dims, jnp.float32) * scale
    if len(shards) > 0:
        values = block_scale(own_key, dims, shards, -0.22, 0.18) * values
    return jnp.clip(values, min=-limit, max=limit).astype(held_as)


def setup_inputs(seed: int = 0) -> dict:
    arg_keys = jax.random.split(jax.random.key(seed), 14)
    return {
        "section_in": draw_section_in(jax.random.fold_in(arg_keys[13], 71), 0),
        "patch_index": touch_ends(jax.random.randint(arg_keys[1], (LAYERS, REQS), 0, PATCHES), jax.random.fold_in(arg_keys[1], 1), 0, PATCHES - 1).astype(jnp.int32),
        "stale_kv": draw_stale_kv(jax.random.fold_in(arg_keys[13], 71), 0),
        "modulation": normal_values(arg_keys[3], (LAYERS, REQS, 6, D), 1.0, 4.0, ((0, 2), (1, 128)), jnp.float32),
        "final_mod": normal_values(arg_keys[4], (REQS, 2, D), 1.0, 4.0, ((0, 128),), jnp.float32),
        "qkv_blocks": draw_qkv_blocks(jax.random.fold_in(arg_keys[13], 71), 0),
        "out_blocks": draw_out_blocks(jax.random.fold_in(arg_keys[13], 71), 0),
        "up_blocks": draw_up_blocks(jax.random.fold_in(arg_keys[13], 71), 0),
        "down_blocks": draw_down_blocks(jax.random.fold_in(arg_keys[13], 71), 0),
        "final_weight": normal_values(arg_keys[9], (D, CH), D ** -0.5, 0.1875),
        "noisy_latent": normal_values(arg_keys[10], (REQS, PATCH_TOK * CH), 1.0, 6.0, ((0, 128), (1, 2)), jnp.float32),
        "time_index": touch_ends(jax.random.randint(arg_keys[11], (REQS,), 100, 500), jax.random.fold_in(arg_keys[11], 1), 100, 499).astype(jnp.int32),
        "time_gap": touch_ends(jax.random.randint(arg_keys[12], (REQS,), 10, 41), jax.random.fold_in(arg_keys[12], 1), 10, 40).astype(jnp.int32),
    }


NORM_EPS = 1e-06
BETA_LOW = 0.0001
BETA_HIGH = 0.02

def layer_norm(values):
    average = lax.optimization_barrier(jnp.mean(values, axis=-1, keepdims=True))
    centred = values - average
    spread = lax.optimization_barrier(jnp.mean(centred * centred, axis=-1, keepdims=True))
    return centred * lax.rsqrt(spread + NORM_EPS)

def alpha_bar(step_index):
    moment = step_index.astype(jnp.float32)
    return jnp.exp(-(BETA_LOW * (moment + 1.0) + (BETA_HIGH - BETA_LOW) * moment * (moment + 1.0) / 1998.0))

def attend(queries, fresh_keys, fresh_values, stale_rows, patch_at):
    fresh_count = queries.shape[0]
    model_width = queries.shape[1]
    head_size = model_width // HEADS
    fresh_rows = jnp.concatenate([fresh_keys, fresh_values], axis=1)
    start = (patch_at * fresh_count).astype(jnp.int32)
    all_rows = lax.dynamic_update_slice(stale_rows, fresh_rows, (start, jnp.zeros((), jnp.int32)))
    key_rows = all_rows[:, :model_width].astype(jnp.float32)
    value_rows = all_rows[:, model_width:].astype(jnp.float32)
    scores = jnp.einsum('qhd,khd->hqk', queries.astype(jnp.float32).reshape(fresh_count, HEADS, head_size), key_rows.reshape(-1, HEADS, head_size)) * head_size ** (-0.5)
    highest = lax.optimization_barrier(jnp.max(scores, axis=-1, keepdims=True))
    raised = jnp.exp(scores - highest)
    attention_weights = (raised / lax.optimization_barrier(jnp.sum(raised, axis=-1, keepdims=True))).astype(jnp.bfloat16)
    mixed = jnp.einsum('hqk,khd->qhd', attention_weights.astype(jnp.float32), value_rows.reshape(-1, HEADS, head_size))
    return mixed.reshape(fresh_count, model_width).astype(jnp.bfloat16)

def layer_step(hidden, stale_rows, mods, patch_at, w_qkv, w_out, w_up, w_down):
    fresh_count = hidden.shape[0]
    model_width = hidden.shape[1]
    residual = hidden.astype(jnp.float32)
    normed = (layer_norm(residual) * (1.0 + mods[1]) + mods[0]).astype(jnp.bfloat16)
    joined = jnp.dot(normed, w_qkv, preferred_element_type=jnp.float32).astype(jnp.bfloat16)
    joined = joined.reshape(fresh_count, UNIT_GROUPS, 3, model_width // UNIT_GROUPS)
    queries = joined[:, :, 0].reshape(fresh_count, model_width)
    fresh_keys = joined[:, :, 1].reshape(fresh_count, model_width)
    fresh_values = joined[:, :, 2].reshape(fresh_count, model_width)
    mixed = attend(queries, fresh_keys, fresh_values, stale_rows, patch_at)
    projected = jnp.dot(mixed, w_out, preferred_element_type=jnp.float32).astype(jnp.bfloat16)
    projected = lax.optimization_barrier(projected)
    after_attention = residual + mods[2] * projected.astype(jnp.float32)
    middle = (layer_norm(after_attention) * (1.0 + mods[4]) + mods[3]).astype(jnp.bfloat16)
    total = jnp.zeros(after_attention.shape, jnp.float32)
    for group in range(UNIT_GROUPS):
        inner = jax.nn.gelu(jnp.dot(middle, w_up[group], preferred_element_type=jnp.float32), approximate=True).astype(jnp.bfloat16)
        partial_out = jnp.dot(inner, w_down[group], preferred_element_type=jnp.float32).astype(jnp.bfloat16)
        partial_out = lax.optimization_barrier(partial_out)
        total = total + partial_out.astype(jnp.float32)
    layer_out = (after_attention + mods[5] * total).astype(jnp.bfloat16)
    return (layer_out, jnp.concatenate([fresh_keys, fresh_values], axis=1))

def reference(section_in, patch_index, stale_kv, modulation, final_mod, qkv_blocks, out_blocks, up_blocks, down_blocks, final_weight, noisy_latent, time_index, time_gap):
    layer_outputs = []
    fresh_all = []
    for layer in range(LAYERS):
        w_qkv = jnp.concatenate([qkv_blocks[layer, group] for group in range(UNIT_GROUPS)], axis=1)
        w_out = jnp.concatenate([out_blocks[layer, group] for group in range(UNIT_GROUPS)], axis=1)
        w_up = up_blocks[layer, :UNIT_GROUPS]
        w_down = down_blocks[layer, :UNIT_GROUPS]

        def one_request(items):
            return layer_step(items[0], items[1], items[2], items[3], w_qkv, w_out, w_up, w_down)
        layer_out, fresh = lax.map(one_request, (section_in[layer], stale_kv[layer], modulation[layer], patch_index[layer]))
        layer_outputs.append(layer_out)
        fresh_all.append(fresh)
    final_rows = layer_outputs[1].astype(jnp.float32)
    shifted = (layer_norm(final_rows) * (1.0 + final_mod[:, 1][:, None, :]) + final_mod[:, 0][:, None, :]).astype(jnp.bfloat16)
    noise_pred = jnp.dot(shifted.reshape(-1, D), final_weight, preferred_element_type=jnp.float32).reshape(REQS, PATCH_TOK * CH)
    now_bar = alpha_bar(time_index)[:, None]
    prev_bar = alpha_bar(time_index - time_gap)[:, None]
    clean_latent = (noisy_latent - jnp.sqrt(1.0 - now_bar) * noise_pred) / jnp.sqrt(now_bar)
    denoised = jnp.sqrt(prev_bar) * clean_latent + jnp.sqrt(1.0 - prev_bar) * noise_pred
    return (jnp.stack(fresh_all), layer_outputs[0], noise_pred, denoised)
```

```python
import functools

import jax
import jax.numpy as jnp
from jax import lax
from jax.experimental import pallas as pl
from jax.experimental.pallas import tpu as pltpu
from jax.sharding import PartitionSpec as P

MESH = pl.DeviceIdType.MESH
HEADS = 16
GROUPS = 4
NORM_EPS = 1e-06
BETA_LOW = 0.0001
BETA_HIGH = 0.02
TOK = 32
D = 1152
BW = D // GROUPS
HEAD = D // HEADS
KEEP = 96
KVW = 640
WIN = 384
RING = 8
F32 = jnp.float32
BF16 = jnp.bfloat16


def layer_norm(values):
    average = jnp.mean(values, axis=-1, keepdims=True)
    centred = values - average
    spread = jnp.mean(centred * centred, axis=-1, keepdims=True)
    return centred * lax.rsqrt(spread + NORM_EPS)


def alpha_bar(moment):
    return jnp.exp(
        -(BETA_LOW * (moment + 1.0) + (BETA_HIGH - BETA_LOW) * moment * (moment + 1.0) / 1998.0)
    )


def kernel(
    patch_ref,
    time_ref,
    gap_ref,
    h_hbm,
    stale_hbm,
    mod_hbm,
    fmod_hbm,
    wq_hbm,
    wo_hbm,
    wu_hbm,
    wd_hbm,
    fw_hbm,
    noisy_hbm,
    fresh_out,
    next_out,
    noise_out,
    den_out,
    h_v,
    st_v,
    mod_v,
    fmod_v,
    wq_v,
    wo_v,
    wu_v,
    wd_v,
    fw_v,
    noisy_v,
    x1,
    x2,
    kvs,
    kvb,
    fk,
    attn_v,
    inner_v,
    ps,
    r2,
    parts,
    r4,
    leave,
    arrive,
    lsem,
    ssem,
    rsem,
):
    s = lax.axis_index("section")
    r = lax.axis_index("req")
    z = lax.rem(r, RING)
    base = r - z
    odd = lax.rem(z, 2)
    mine = lax.rem(z, GROUPS)

    def at(dz):
        return (s, base + lax.rem(z + dz + RING, RING))

    far = 2 - 4 * odd
    outward = [
        (at(1), lax.rem(z + 1, GROUPS), 2),
        (at(-1), lax.rem(z + 3, GROUPS), 1),
        (at(far), lax.rem(z + 2, GROUPS), 3),
    ]
    homeward = [(1, at(1), 2), (2, at(-1), 1), (3, at(-far), 3)]
    other = (1 - s, r)

    local = []

    def load(i, src, dst):
        copy = pltpu.make_async_copy(src, dst, lsem.at[i])
        copy.start()
        local.append(copy)
        return copy

    c_h = load(0, h_hbm, h_v)
    c_mod = load(1, mod_hbm, mod_v)
    c_st = load(2, stale_hbm, st_v)
    c_wq = load(3, wq_hbm, wq_v)

    barrier = pltpu.get_barrier_semaphore()
    for peer in (at(1), at(-1), at(2), at(-2), other):
        pl.semaphore_signal(barrier, inc=1, device_id=peer, device_id_type=MESH)

    wo_v[:, 0:TOK, :] = jnp.zeros((GROUPS, TOK, BW), BF16)
    wo_v[:, TOK + BW :, :] = jnp.zeros((GROUPS, WIN - TOK - BW, BW), BF16)
    c_wo = load(4, wo_hbm.at[pl.ds(mine * BW, BW), :], wo_v.at[mine, pl.ds(TOK, BW), :])
    c_wu = load(5, wu_hbm, wu_v)
    c_wd = load(6, wd_hbm, wd_v)
    c_fw = load(7, fw_hbm, fw_v)
    c_fm = load(8, fmod_hbm, fmod_v)
    c_nz = load(9, noisy_hbm, noisy_v)

    sends = []
    count = [0]

    def remote(src, dst, device):
        i = count[0]
        count[0] += 1
        copy = pltpu.make_async_remote_copy(
            src_ref=src,
            dst_ref=dst,
            send_sem=ssem.at[i],
            recv_sem=rsem.at[i],
            device_id=device,
            device_id_type=MESH,
        )
        copy.start()
        sends.append(copy)
        return copy

    c_h.wait()
    c_mod.wait()
    normed = layer_norm(h_v[...].astype(F32)) * (1.0 + mod_v[1:2, :]) + mod_v[0:1, :]
    x1[0] = normed.astype(BF16)

    c_st.wait()
    patch = patch_ref[0, 0]
    for k in range(3):
        low = st_v[k * TOK : (k + 1) * TOK, :].astype(F32)
        high = st_v[(k + 1) * TOK : (k + 2) * TOK, :].astype(F32)
        kept = jnp.where(patch <= k, high, low)
        for j in range(GROUPS):
            kvs[j, k * TOK : (k + 1) * TOK, :] = jnp.concatenate(
                [
                    kept[:, j * BW : (j + 1) * BW],
                    kept[:, D + j * BW : D + (j + 1) * BW],
                    jnp.zeros((TOK, KVW - 2 * BW), F32),
                ],
                axis=1,
            ).astype(BF16)
    kvb[0, 0:KEEP, :] = kvs[mine]

    pl.semaphore_wait(barrier, 5)
    c_x = [remote(x1.at[0], x1.at[slot], dev) for dev, _, slot in outward]
    c_kv = [
        remote(kvs.at[res], kvb.at[slot, pl.ds(0, KEEP), :], dev) for dev, res, slot in outward
    ]
    c_w = [
        remote(
            wo_hbm.at[pl.ds(res * BW, BW), :],
            wo_v.at[mine, pl.ds(TOK, BW), :],
            dev,
        )
        for dev, res, _ in outward
    ]

    c_wq.wait()
    for c in c_x:
        c.wait_recv()
    qkv = jnp.dot(x1[...].reshape(GROUPS * TOK, D), wq_v[...], preferred_element_type=F32)
    fresh = jnp.concatenate(
        [qkv[:, BW:], jnp.zeros((GROUPS * TOK, KVW - 2 * BW), F32)], axis=1
    ).astype(BF16)
    for slot in range(GROUPS):
        kvb[slot, KEEP:, :] = fresh[slot * TOK : (slot + 1) * TOK]
    fk[mine] = fresh[0:TOK]
    c_f = [
        remote(kvb.at[slot, pl.ds(KEEP, TOK), :], fk.at[mine], dev) for slot, dev, _ in homeward
    ]

    q_lane = lax.broadcasted_iota(jnp.int32, (TOK, WIN), 1)
    for c in c_kv:
        c.wait_recv()
    for slot in range(GROUPS):
        q = qkv[slot * TOK : (slot + 1) * TOK, 0:WIN]
        spread = jnp.concatenate(
            [
                jnp.where((q_lane >= a * HEAD) & (q_lane < (a + 1) * HEAD), q, 0.0)
                for a in range(HEADS // GROUPS)
            ],
            axis=0,
        ).astype(BF16)
        scores = lax.dot_general(
            spread, kvb[slot, :, 0:WIN], (((1,), (1,)), ((), ())), preferred_element_type=F32
        ) * HEAD ** (-0.5)
        raised = jnp.exp(scores - jnp.max(scores, axis=-1, keepdims=True))
        probs = (raised / jnp.sum(raised, axis=-1, keepdims=True)).astype(BF16)
        mixed = jnp.dot(probs, kvb[slot, :, 256:KVW], preferred_element_type=F32)
        picked = jnp.zeros((TOK, WIN), F32)
        for a in range(HEADS // GROUPS):
            low = TOK + a * HEAD
            picked = jnp.where(
                (q_lane >= low) & (q_lane < low + HEAD), mixed[a * TOK : (a + 1) * TOK], picked
            )
        attn_v[slot * TOK : (slot + 1) * TOK, :] = picked.astype(BF16)

    c_wo.wait()
    for c in c_w:
        c.wait_recv()
    attn = attn_v[...]
    partial = jnp.concatenate(
        [jnp.dot(attn, wo_v[j], preferred_element_type=F32) for j in range(GROUPS)], axis=1
    )
    for slot in range(1, GROUPS):
        ps[slot - 1] = partial[slot * TOK : (slot + 1) * TOK].astype(BF16)
    c_p = [remote(ps.at[slot - 1], r2.at[i - 1], dev) for slot, dev, i in homeward]

    for c in c_f:
        c.wait_recv()
    for j in range(GROUPS):
        block = fk[j].astype(F32)
        fk_k = block[:, 0:BW]
        fk_v = block[:, BW : 2 * BW]
        if j == 0:
            keys, vals = [fk_k], [fk_v]
        else:
            keys.append(fk_k)
            vals.append(fk_v)
    fresh_out[...] = jnp.concatenate(keys + vals, axis=1).astype(BF16)
    c_fw.wait()
    channels = fw_v.shape[1]
    spots = (TOK // 2) * channels
    tile_row = lax.broadcasted_iota(jnp.int32, (channels, spots), 0)
    tile_col = lax.broadcasted_iota(jnp.int32, (channels, spots), 1)
    copies = (lax.rem(tile_col, channels) == tile_row).astype(BF16)
    fw_tiled = jnp.dot(fw_v[...], copies, preferred_element_type=F32).astype(BF16)

    for c in c_p:
        c.wait_recv()
    proj = partial[0:TOK]
    for i in range(GROUPS - 1):
        proj = proj + r2[i].astype(F32)
    h1 = h_v[...].astype(F32) + mod_v[2:3, :] * proj
    middle = layer_norm(h1) * (1.0 + mod_v[4:5, :]) + mod_v[3:4, :]
    x2[0] = middle.astype(BF16)
    c_m = [remote(x2.at[0], x2.at[slot], dev) for dev, _, slot in outward]
    c_wu.wait()
    c_wd.wait()
    for c in c_m:
        c.wait_recv()
    inner_v[...] = jax.nn.gelu(
        jnp.dot(x2[...].reshape(GROUPS * TOK, D), wu_v[...], preferred_element_type=F32),
        approximate=True,
    ).astype(BF16)
    part = jnp.dot(inner_v[...], wd_v[...], preferred_element_type=F32)
    for slot in range(1, GROUPS):
        parts[slot - 1] = part[slot * TOK : (slot + 1) * TOK].astype(BF16)
    c_d = [remote(parts.at[slot - 1], r4.at[i - 1], dev) for slot, dev, i in homeward]
    for c in c_d:
        c.wait_recv()
    total = part[0:TOK]
    for i in range(GROUPS - 1):
        total = total + r4[i].astype(F32)
    layer_out = (h1 + mod_v[5:6, :] * total).astype(BF16)

    half = TOK // 2
    upper = layer_out[:half]
    lower = layer_out[half:]
    first = s == 0
    leave[...] = jnp.where(first, lower, upper)
    c_a = remote(leave, arrive, other)
    c_fm.wait()
    c_nz.wait()
    c_a.wait_recv()
    arrived = arrive[...]
    next_out[...] = jnp.where(first, upper, arrived)
    final_rows = jnp.where(first, arrived, lower).astype(F32)
    shifted = (layer_norm(final_rows) * (1.0 + fmod_v[1:2, :]) + fmod_v[0:1, :]).astype(BF16)
    each = jnp.dot(shifted, fw_tiled, preferred_element_type=F32)
    row = lax.broadcasted_iota(jnp.int32, (half, spots), 0)
    col = lax.broadcasted_iota(jnp.int32, (half, spots), 1)
    noise = jnp.sum(jnp.where(lax.div(col, channels) == row, each, 0.0), axis=0, keepdims=True)
    now = jnp.full((1, spots), time_ref[0], jnp.int32)
    before = jnp.full((1, spots), time_ref[0] - gap_ref[0], jnp.int32)
    now_bar = alpha_bar(now.astype(F32))
    prev_bar = alpha_bar(before.astype(F32))
    clean = (noisy_v[...] - jnp.sqrt(1.0 - now_bar) * noise) / jnp.sqrt(now_bar)
    noise_out[...] = noise
    den_out[...] = jnp.sqrt(prev_bar) * clean + jnp.sqrt(1.0 - prev_bar) * noise

    for c in sends:
        c.wait_send()


def per_device(
    section_in,
    patch_index,
    stale_kv,
    modulation,
    final_mod,
    qkv_blocks,
    out_blocks,
    up_blocks,
    down_blocks,
    final_weight,
    noisy_latent,
    time_index,
    time_gap,
):
    any_spec = pl.BlockSpec(memory_space=pl.ANY)
    smem = pl.BlockSpec(memory_space=pltpu.SMEM)
    vmem = pl.BlockSpec(memory_space=pltpu.VMEM)
    spots = noisy_latent.shape[1]
    remote_count = 22
    fresh, next_rows, noise_pred, denoised = pl.pallas_call(
        kernel,
        name="relay_step",
        out_shape=(
            jax.ShapeDtypeStruct((TOK, 2 * D), BF16),
            jax.ShapeDtypeStruct((TOK // 2, D), BF16),
            jax.ShapeDtypeStruct((1, spots), F32),
            jax.ShapeDtypeStruct((1, spots), F32),
        ),
        in_specs=[smem] * 3 + [any_spec] * 10,
        out_specs=(vmem,) * 4,
        scratch_shapes=[
            pltpu.VMEM((TOK, D), BF16),
            pltpu.VMEM((4 * TOK, 2 * D), BF16),
            pltpu.VMEM((6, D), F32),
            pltpu.VMEM((2, D), F32),
            pltpu.VMEM((D, 3 * BW), BF16),
            pltpu.VMEM((GROUPS, WIN, BW), BF16),
            pltpu.VMEM((D, D), BF16),
            pltpu.VMEM((D, D), BF16),
            pltpu.VMEM(final_weight.shape, BF16),
            pltpu.VMEM((1, spots), F32),
            pltpu.VMEM((GROUPS, TOK, D), BF16),
            pltpu.VMEM((GROUPS, TOK, D), BF16),
            pltpu.VMEM((GROUPS, KEEP, KVW), BF16),
            pltpu.VMEM((GROUPS, KEEP + TOK, KVW), BF16),
            pltpu.VMEM((GROUPS, TOK, KVW), BF16),
            pltpu.VMEM((GROUPS * TOK, WIN), BF16),
            pltpu.VMEM((GROUPS * TOK, D), BF16),
            pltpu.VMEM((GROUPS - 1, TOK, D), BF16),
            pltpu.VMEM((GROUPS - 1, TOK, D), BF16),
            pltpu.VMEM((GROUPS - 1, TOK, D), BF16),
            pltpu.VMEM((GROUPS - 1, TOK, D), BF16),
            pltpu.VMEM((TOK // 2, D), BF16),
            pltpu.VMEM((TOK // 2, D), BF16),
            pltpu.SemaphoreType.DMA((10,)),
            pltpu.SemaphoreType.DMA((remote_count,)),
            pltpu.SemaphoreType.DMA((remote_count,)),
        ],
        compiler_params=pltpu.CompilerParams(
            collective_id=0, has_side_effects=True, vmem_limit_bytes=48 * 1024 * 1024
        ),
    )(
        patch_index,
        time_index,
        time_gap,
        section_in[0, 0],
        stale_kv[0, 0],
        modulation[0, 0],
        final_mod[0],
        qkv_blocks[0, 0],
        out_blocks[0, 0],
        up_blocks[0, 0],
        down_blocks[0, 0],
        final_weight,
        noisy_latent,
    )
    return (fresh[None, None], next_rows[None], noise_pred, denoised)


def solution(mesh):
    placed = (
        P("section", "req", None, None),
        P("section", "req"),
        P("section", "req", None, None),
        P("section", "req", None, None),
        P("req", None, None),
        P("section", "req", None, None),
        P("section", "req", None, None),
        P("section", "req", None, None),
        P("section", "req", None, None),
        P(),
        P("req", "section"),
        P("req"),
        P("req"),
    )
    return jax.shard_map(
        per_device,
        mesh=mesh,
        in_specs=placed,
        out_specs=(
            P("section", "req", None, None),
            P("req", "section", None),
            P("req", "section"),
            P("req", "section"),
        ),
        check_vma=False,
    )
```

```python
import functools

import jax
import jax.numpy as jnp
from jax import lax
from jax.experimental import pallas as pl
from jax.experimental.pallas import tpu as pltpu
from jax.sharding import PartitionSpec as P

MESH = pl.DeviceIdType.MESH
HEADS = 16
GROUPS = 4
NORM_EPS = 1e-06
BETA_LOW = 0.0001
BETA_HIGH = 0.02
TOK = 32
D = 1152
BW = D // GROUPS
HEAD = D // HEADS
KEEP = 96
KVW = 640
WIN = 384
RING = 8
F32 = jnp.float32
BF16 = jnp.bfloat16


def layer_norm(values):
    average = jnp.mean(values, axis=-1, keepdims=True)
    centred = values - average
    spread = jnp.mean(centred * centred, axis=-1, keepdims=True)
    return centred * lax.rsqrt(spread + NORM_EPS)


def dot_t(a, b):
    return lax.dot_general(a, b, (((1,), (1,)), ((), ())), preferred_element_type=F32)


def alpha_bar(moment):
    return jnp.exp(
        -(BETA_LOW * (moment + 1.0) + (BETA_HIGH - BETA_LOW) * moment * (moment + 1.0) / 1998.0)
    )


def kernel(
    patch_hbm,
    time_hbm,
    gap_hbm,
    h_hbm,
    stale_hbm,
    mod_hbm,
    fmod_hbm,
    wq_hbm,
    wo_hbm,
    wu_hbm,
    wd_hbm,
    fw_hbm,
    noisy_hbm,
    fresh_out,
    next_out,
    noise_out,
    den_out,
    patch_ref,
    time_ref,
    gap_ref,
    h_v,
    st_v,
    mod_v,
    fmod_v,
    wq_v,
    wo_v,
    wu_v,
    wd_v,
    fw_v,
    noisy_v,
    x1,
    x2,
    kvs,
    kvb,
    fk,
    attn_v,
    inner_v,
    ps,
    r2,
    parts,
    r4,
    leave,
    arrive,
    lsem,
    ssem,
    rsem,
):
    s = lax.axis_index("section")
    r = lax.axis_index("req")
    z = lax.rem(r, RING)
    base = r - z
    odd = lax.rem(z, 2)
    mine = lax.rem(z, GROUPS)

    def at(dz):
        return (s, base + lax.rem(z + dz + RING, RING))

    far = 2 - 4 * odd
    outward = [
        (at(1), lax.rem(z + 1, GROUPS), 2),
        (at(-1), lax.rem(z + 3, GROUPS), 1),
        (at(far), lax.rem(z + 2, GROUPS), 3),
    ]
    homeward = [(1, at(1), 2), (2, at(-1), 1), (3, at(-far), 3)]
    other = (1 - s, r)

    local = []

    def load(i, src, dst):
        copy = pltpu.make_async_copy(src, dst, lsem.at[i])
        copy.start()
        local.append(copy)
        return copy

    c_h = load(0, h_hbm, h_v)
    c_mod = load(1, mod_hbm, mod_v)
    c_st = load(2, stale_hbm, st_v)
    c_pt = load(10, patch_hbm, patch_ref)
    c_wq = load(3, wq_hbm, wq_v)

    barrier = pltpu.get_barrier_semaphore()
    for peer in (at(1), at(-1), at(2), at(-2), other):
        pl.semaphore_signal(barrier, inc=1, device_id=peer, device_id_type=MESH)

    def heads_rows(j):
        return wo_hbm.at[:, pl.ds(pl.multiple_of(j * 256, 256), WIN)]

    c_wo = load(4, heads_rows(mine), wo_v.at[mine])
    c_wu = load(5, wu_hbm, wu_v)
    c_wd = load(6, wd_hbm, wd_v)
    c_fw = load(7, fw_hbm, fw_v)
    c_fm = load(8, fmod_hbm, fmod_v)
    c_nz = load(9, noisy_hbm, noisy_v)
    c_tm = load(11, time_hbm, time_ref)
    c_gp = load(12, gap_hbm, gap_ref)

    sends = []
    count = [0]

    def remote(src, dst, device):
        i = count[0]
        count[0] += 1
        copy = pltpu.make_async_remote_copy(
            src_ref=src,
            dst_ref=dst,
            send_sem=ssem.at[i],
            recv_sem=rsem.at[i],
            device_id=device,
            device_id_type=MESH,
        )
        copy.start()
        sends.append(copy)
        return copy

    c_h.wait()
    c_mod.wait()
    normed = layer_norm(h_v[...].astype(F32)) * (1.0 + mod_v[1]) + mod_v[0]
    x1[0] = normed.astype(BF16)

    c_st.wait()
    c_pt.wait()
    patch = patch_ref[0, 0]
    for k in range(3):
        low = st_v[k * TOK : (k + 1) * TOK, :].astype(F32)
        high = st_v[(k + 1) * TOK : (k + 2) * TOK, :].astype(F32)
        kept = jnp.where(patch <= k, high, low)
        for j in range(GROUPS):
            kvs[j, k * TOK : (k + 1) * TOK, :] = jnp.concatenate(
                [
                    kept[:, j * BW : (j + 1) * BW],
                    kept[:, D + j * BW : D + (j + 1) * BW],
                    jnp.zeros((TOK, KVW - 2 * BW), F32),
                ],
                axis=1,
            ).astype(BF16)
    kvb[0, 0:KEEP, :] = kvs[mine]

    pl.semaphore_wait(barrier, 5)
    c_x = [remote(x1.at[0], x1.at[slot], dev) for dev, _, slot in outward]
    c_kv = [
        remote(kvs.at[res], kvb.at[slot, pl.ds(0, KEEP), :], dev) for dev, res, slot in outward
    ]
    c_w = [
        remote(heads_rows(res), wo_v.at[mine], dev)
        for dev, res, _ in outward
    ]

    c_wq.wait()
    for c in c_x:
        c.wait_recv()
    qkv = dot_t(x1[...].reshape(GROUPS * TOK, D), wq_v[...])
    fresh = jnp.concatenate(
        [qkv[:, BW:], jnp.zeros((GROUPS * TOK, KVW - 2 * BW), F32)], axis=1
    ).astype(BF16)
    for slot in range(GROUPS):
        kvb[slot, KEEP:, :] = fresh[slot * TOK : (slot + 1) * TOK]
    fk[mine] = fresh[0:TOK]
    c_f = [
        remote(kvb.at[slot, pl.ds(KEEP, TOK), :], fk.at[mine], dev) for slot, dev, _ in homeward
    ]

    q_lane = lax.broadcasted_iota(jnp.int32, (TOK, WIN), 1)
    for c in c_kv:
        c.wait_recv()
    for slot in range(GROUPS):
        q = qkv[slot * TOK : (slot + 1) * TOK, 0:WIN]
        spread = jnp.concatenate(
            [
                jnp.where((q_lane >= a * HEAD) & (q_lane < (a + 1) * HEAD), q, 0.0)
                for a in range(HEADS // GROUPS)
            ],
            axis=0,
        ).astype(BF16)
        scores = dot_t(spread, kvb[slot, :, 0:WIN]) * HEAD ** (-0.5)
        raised = jnp.exp(scores - jnp.max(scores, axis=-1, keepdims=True))
        probs = (raised / jnp.sum(raised, axis=-1, keepdims=True)).astype(BF16)
        mixed = jnp.dot(probs, kvb[slot, :, 256:KVW], preferred_element_type=F32)
        picked = jnp.zeros((TOK, WIN), F32)
        for a in range(HEADS // GROUPS):
            low = TOK + a * HEAD
            picked = jnp.where(
                (q_lane >= low) & (q_lane < low + HEAD), mixed[a * TOK : (a + 1) * TOK], picked
            )
        shift = lax.rem(TOK * (mine + WIN // TOK - 1), WIN)
        attn_v[slot * TOK : (slot + 1) * TOK, :] = pltpu.roll(picked, shift, 1).astype(BF16)

    c_wo.wait()
    for c in c_w:
        c.wait_recv()
    attn = attn_v[...]
    partial = jnp.concatenate(
        [dot_t(attn, wo_v[j]) for j in range(GROUPS)], axis=1
    )
    for slot in range(1, GROUPS):
        ps[slot - 1] = partial[slot * TOK : (slot + 1) * TOK].astype(BF16)
    c_p = [remote(ps.at[slot - 1], r2.at[i - 1], dev) for slot, dev, i in homeward]

    for c in c_f:
        c.wait_recv()
    for j in range(GROUPS):
        block = fk[j].astype(F32)
        fk_k = block[:, 0:BW]
        fk_v = block[:, BW : 2 * BW]
        if j == 0:
            keys, vals = [fk_k], [fk_v]
        else:
            keys.append(fk_k)
            vals.append(fk_v)
    fresh_out[...] = jnp.concatenate(keys + vals, axis=1).astype(BF16)
    c_fw.wait()
    channels = fw_v.shape[0]
    spots = (TOK // 2) * channels
    fw_tiled = jnp.concatenate([fw_v[...]] * (TOK // 2), axis=0)

    for c in c_p:
        c.wait_recv()
    proj = partial[0:TOK]
    for i in range(GROUPS - 1):
        proj = proj + r2[i].astype(F32)
    h1 = h_v[...].astype(F32) + mod_v[2] * proj
    middle = layer_norm(h1) * (1.0 + mod_v[4]) + mod_v[3]
    x2[0] = middle.astype(BF16)
    c_m = [remote(x2.at[0], x2.at[slot], dev) for dev, _, slot in outward]
    c_wu.wait()
    c_wd.wait()
    for c in c_m:
        c.wait_recv()
    inner_v[...] = jax.nn.gelu(
        jnp.dot(x2[...].reshape(GROUPS * TOK, D), wu_v[...], preferred_element_type=F32),
        approximate=True,
    ).astype(BF16)
    part = jnp.dot(inner_v[...], wd_v[...], preferred_element_type=F32)
    for slot in range(1, GROUPS):
        parts[slot - 1] = part[slot * TOK : (slot + 1) * TOK].astype(BF16)
    c_d = [remote(parts.at[slot - 1], r4.at[i - 1], dev) for slot, dev, i in homeward]
    for c in c_d:
        c.wait_recv()
    total = part[0:TOK]
    for i in range(GROUPS - 1):
        total = total + r4[i].astype(F32)
    layer_out = (h1 + mod_v[5] * total).astype(BF16)

    half = TOK // 2
    upper = layer_out[:half]
    lower = layer_out[half:]
    first = s == 0
    leave[...] = jnp.where(first, lower, upper)
    c_a = remote(leave, arrive, other)
    c_fm.wait()
    c_nz.wait()
    c_tm.wait()
    c_gp.wait()
    c_a.wait_recv()
    arrived = arrive[...]
    next_out[...] = jnp.where(first, upper, arrived)
    final_rows = jnp.where(first, arrived, lower).astype(F32)
    shifted = (layer_norm(final_rows) * (1.0 + fmod_v[1:2, :]) + fmod_v[0:1, :]).astype(BF16)
    each = dot_t(shifted, fw_tiled)
    row = lax.broadcasted_iota(jnp.int32, (half, spots), 0)
    col = lax.broadcasted_iota(jnp.int32, (half, spots), 1)
    noise = jnp.sum(jnp.where(lax.div(col, channels) == row, each, 0.0), axis=0, keepdims=True)
    now = jnp.full((1, spots), time_ref[0], jnp.int32)
    before = jnp.full((1, spots), time_ref[0] - gap_ref[0], jnp.int32)
    now_bar = alpha_bar(now.astype(F32))
    prev_bar = alpha_bar(before.astype(F32))
    clean = (noisy_v[...] - jnp.sqrt(1.0 - now_bar) * noise) / jnp.sqrt(now_bar)
    noise_out[...] = noise
    den_out[...] = jnp.sqrt(prev_bar) * clean + jnp.sqrt(1.0 - prev_bar) * noise

    for c in sends:
        c.wait_send()


def per_device(
    section_in,
    patch_index,
    stale_kv,
    modulation,
    final_mod,
    qkv_blocks,
    out_blocks,
    up_blocks,
    down_blocks,
    final_weight,
    noisy_latent,
    time_index,
    time_gap,
):
    any_spec = pl.BlockSpec(memory_space=pltpu.HBM)
    vmem = pl.BlockSpec(memory_space=pltpu.VMEM)
    spots = noisy_latent.shape[1]
    remote_count = 22
    fresh, next_rows, noise_pred, denoised = pl.pallas_call(
        kernel,
        name="relay_step",
        out_shape=(
            jax.ShapeDtypeStruct((TOK, 2 * D), BF16),
            jax.ShapeDtypeStruct((TOK // 2, D), BF16),
            jax.ShapeDtypeStruct((1, spots), F32),
            jax.ShapeDtypeStruct((1, spots), F32),
        ),
        in_specs=[any_spec] * 13,
        out_specs=(vmem,) * 4,
        scratch_shapes=[
            pltpu.SMEM((1, 1), jnp.int32),
            pltpu.SMEM((1,), jnp.int32),
            pltpu.SMEM((1,), jnp.int32),
            pltpu.VMEM((TOK, D), BF16),
            pltpu.VMEM((4 * TOK, 2 * D), BF16),
            pltpu.VMEM((6, 1, D), F32),
            pltpu.VMEM((2, D), F32),
            pltpu.VMEM((3 * BW, D), BF16),
            pltpu.VMEM((GROUPS, BW, WIN), BF16),
            pltpu.VMEM((D, D), BF16),
            pltpu.VMEM((D, D), BF16),
            pltpu.VMEM(final_weight.shape[::-1], BF16),
            pltpu.VMEM((1, spots), F32),
            pltpu.VMEM((GROUPS, TOK, D), BF16),
            pltpu.VMEM((GROUPS, TOK, D), BF16),
            pltpu.VMEM((GROUPS, KEEP, KVW), BF16),
            pltpu.VMEM((GROUPS, KEEP + TOK, KVW), BF16),
            pltpu.VMEM((GROUPS, TOK, KVW), BF16),
            pltpu.VMEM((GROUPS * TOK, WIN), BF16),
            pltpu.VMEM((GROUPS * TOK, D), BF16),
            pltpu.VMEM((GROUPS - 1, TOK, D), BF16),
            pltpu.VMEM((GROUPS - 1, TOK, D), BF16),
            pltpu.VMEM((GROUPS - 1, TOK, D), BF16),
            pltpu.VMEM((GROUPS - 1, TOK, D), BF16),
            pltpu.VMEM((TOK // 2, D), BF16),
            pltpu.VMEM((TOK // 2, D), BF16),
            pltpu.SemaphoreType.DMA((13,)),
            pltpu.SemaphoreType.DMA((remote_count,)),
            pltpu.SemaphoreType.DMA((remote_count,)),
        ],
        compiler_params=pltpu.CompilerParams(
            collective_id=0, has_side_effects=True, vmem_limit_bytes=63 * 1024 * 1024
        ),
    )(
        patch_index,
        time_index,
        time_gap,
        section_in[0, 0],
        stale_kv[0, 0],
        modulation[0, 0][:, None, :],
        final_mod[0],
        qkv_blocks[0, 0].T,
        out_blocks[0, 0].T,
        up_blocks[0, 0],
        down_blocks[0, 0],
        final_weight.T,
        noisy_latent,
    )
    return (fresh[None, None], next_rows[None], noise_pred, denoised)


def solution(mesh):
    placed = (
        P("section", "req", None, None),
        P("section", "req"),
        P("section", "req", None, None),
        P("section", "req", None, None),
        P("req", None, None),
        P("section", "req", None, None),
        P("section", "req", None, None),
        P("section", "req", None, None),
        P("section", "req", None, None),
        P(),
        P("req", "section"),
        P("req"),
        P("req"),
    )
    return jax.shard_map(
        per_device,
        mesh=mesh,
        in_specs=placed,
        out_specs=(
            P("section", "req", None, None),
            P("req", "section", None),
            P("req", "section"),
            P("req", "section"),
        ),
        check_vma=False,
    )
```

```python
import functools

import jax
import jax.numpy as jnp
from jax import lax
from jax.experimental import pallas as pl
from jax.experimental.pallas import tpu as pltpu
from jax.sharding import PartitionSpec as P

MESH = pl.DeviceIdType.MESH
HEADS = 16
GROUPS = 4
NORM_EPS = 1e-06
BETA_LOW = 0.0001
BETA_HIGH = 0.02
TOK = 32
HALF = TOK // 2
D = 1152
BW = D // GROUPS
HEAD = D // HEADS
KEEP = 96
WIN = 384
RING = 8
F32 = jnp.float32
BF16 = jnp.bfloat16


def layer_norm(values):
    average = jnp.mean(values, axis=-1, keepdims=True)
    centred = values - average
    spread = jnp.mean(centred * centred, axis=-1, keepdims=True)
    return centred * lax.rsqrt(spread + NORM_EPS)


def dot_t(a, b):
    return lax.dot_general(a, b, (((1,), (1,)), ((), ())), preferred_element_type=F32)


def alpha_bar(moment):
    return jnp.exp(
        -(BETA_LOW * (moment + 1.0) + (BETA_HIGH - BETA_LOW) * moment * (moment + 1.0) / 1998.0)
    )


def kernel(
    patch_hbm,
    time_hbm,
    gap_hbm,
    h_hbm,
    stale_hbm,
    mod_hbm,
    fmod_hbm,
    wq_hbm,
    wo_hbm,
    wu_hbm,
    wd_hbm,
    fw_hbm,
    noisy_hbm,
    fresh_out,
    next_out,
    noise_out,
    den_out,
    patch_ref,
    time_ref,
    gap_ref,
    h_v,
    st_v,
    mod_v,
    fmod_v,
    wq_v,
    wo_v,
    wu_v,
    wd_v,
    fw_v,
    noisy_v,
    x1,
    qs,
    qr,
    kv,
    x2,
    ps,
    pr,
    x3,
    inner_v,
    parts,
    r4,
    leave,
    arrive,
    lsem,
    ssem,
    rsem,
):
    s = lax.axis_index("section")
    r = lax.axis_index("req")
    z = lax.rem(r, RING)
    base = r - z
    odd = lax.rem(z, 2)
    mine = lax.rem(z, GROUPS)

    def at(dz):
        return (s, base + lax.rem(z + dz + RING, RING))

    far = 2 - 4 * odd
    outward = [(at(far), 3), (at(1), 2), (at(-1), 1)]
    homeward = [(3, at(-far), 3), (1, at(1), 2), (2, at(-1), 1)]
    other = (1 - s, r)
    rows = [pl.multiple_of(HALF * (1 - s), HALF), pl.multiple_of(HALF * s, HALF)]
    halves = (0, 1)

    local = []

    def load(i, src, dst):
        copy = pltpu.make_async_copy(src, dst, lsem.at[i])
        copy.start()
        local.append(copy)
        return copy

    c_h = load(0, h_hbm, h_v)
    c_mod = load(1, mod_hbm, mod_v)
    barrier = pltpu.get_barrier_semaphore()
    for peer in (at(1), at(-1), at(2), at(-2), other):
        pl.semaphore_signal(barrier, inc=1, device_id=peer, device_id_type=MESH)
    c_wq = load(3, wq_hbm, wq_v)
    c_pt = load(10, patch_hbm, patch_ref)
    c_st = load(2, stale_hbm, st_v)
    c_wo = load(4, wo_hbm, wo_v)
    c_wu = load(5, wu_hbm, wu_v)
    c_wd = load(6, wd_hbm, wd_v)
    c_fw = load(7, fw_hbm, fw_v)
    c_fm = load(8, fmod_hbm, fmod_v)
    c_nz = load(9, noisy_hbm, noisy_v)
    c_tm = load(11, time_hbm, time_ref)
    c_gp = load(12, gap_hbm, gap_ref)

    sends = []
    count = [0]

    def remote(src, dst, device):
        i = count[0]
        count[0] += 1
        copy = pltpu.make_async_remote_copy(
            src_ref=src,
            dst_ref=dst,
            send_sem=ssem.at[i],
            recv_sem=rsem.at[i],
            device_id=device,
            device_id_type=MESH,
        )
        copy.start()
        sends.append(copy)
        return copy

    def spread_tokens(buf, o):
        return [remote(buf.at[o, 0], buf.at[o, slot], dev) for dev, slot in outward]

    def arrive_all(copies):
        for c in copies:
            c.wait_recv()

    c_h.wait()
    c_mod.wait()
    normed = layer_norm(h_v[...].astype(F32)) * (1.0 + mod_v[1]) + mod_v[0]
    flip = s == 0
    x1[0, 0] = jnp.where(flip, normed[HALF:], normed[:HALF]).astype(BF16)
    x1[1, 0] = jnp.where(flip, normed[:HALF], normed[HALF:]).astype(BF16)

    pl.semaphore_wait(barrier, 5)
    c_x = [spread_tokens(x1, o) for o in halves]

    c_st.wait()
    c_pt.wait()
    patch = patch_ref[0, 0]
    for k in range(3):
        low = st_v[k * TOK : (k + 1) * TOK, :]
        high = st_v[(k + 1) * TOK : (k + 2) * TOK, :]
        kv[k * TOK : (k + 1) * TOK, :] = jnp.where(patch <= k, high, low)

    c_wq.wait()
    c_q = []
    for o in halves:
        arrive_all(c_x[o])
        qkv = dot_t(x1[o].reshape(GROUPS * HALF, D), wq_v[...]).astype(BF16)
        qs[o] = qkv.reshape(GROUPS, HALF, 3 * BW)
        c_q.append([remote(qs.at[o, slot], qr.at[o, mine], dev) for slot, dev, _ in homeward])
        qr[o, mine] = qkv[0:HALF]

    queries = []
    for o in halves:
        arrive_all(c_q[o])
        blocks = [qr[o, j].astype(F32) for j in range(GROUPS)]
        queries.append(jnp.concatenate([b[:, 0:BW] for b in blocks], axis=1))
        fresh = jnp.concatenate(
            [b[:, BW : 2 * BW] for b in blocks] + [b[:, 2 * BW :] for b in blocks], axis=1
        )
        kv[pl.ds(KEEP + rows[o], HALF), :] = fresh.astype(BF16)

    lane = lax.broadcasted_iota(jnp.int32, (HALF, WIN), 1)
    c_wo.wait()
    c_m = []
    for o in halves:
        wins = []
        for j in range(GROUPS):
            q = queries[o][:, 256 * j : 256 * j + WIN]
            masks = [
                (lane >= TOK * j + a * HEAD) & (lane < TOK * j + (a + 1) * HEAD)
                for a in range(HEADS // GROUPS)
            ]
            spread = jnp.concatenate([jnp.where(m, q, 0.0) for m in masks], axis=0).astype(BF16)
            scores = dot_t(spread, kv[:, 256 * j : 256 * j + WIN]) * HEAD ** (-0.5)
            raised = jnp.exp(scores - jnp.max(scores, axis=-1, keepdims=True))
            probs = (raised / jnp.sum(raised, axis=-1, keepdims=True)).astype(BF16)
            mixed = jnp.dot(
                probs, kv[:, D + 256 * j : D + 256 * j + WIN], preferred_element_type=F32
            )
            picked = jnp.zeros((HALF, WIN), F32)
            for a, m in enumerate(masks):
                picked = jnp.where(m, mixed[a * HALF : (a + 1) * HALF], picked)
            wins.append(picked)
        cuts = [wins[0][:, 0:256]]
        for j in range(1, GROUPS):
            cuts.append(wins[j - 1][:, 256:WIN] + wins[j][:, 0:128])
            cuts.append(wins[j][:, 128:256])
        cuts.append(wins[GROUPS - 1][:, 256:WIN])
        x2[o, 0] = jnp.concatenate(cuts, axis=1).astype(BF16)
        c_m.append(spread_tokens(x2, o))

    c_p = []
    for o in halves:
        arrive_all(c_m[o])
        proj = dot_t(x2[o].reshape(GROUPS * HALF, D), wo_v[...]).astype(BF16)
        ps[o] = proj.reshape(GROUPS, HALF, BW)
        c_p.append([remote(ps.at[o, slot], pr.at[o, mine], dev) for slot, dev, _ in homeward])
        pr[o, mine] = proj[0:HALF]

    c_u = []
    kept = []
    for o in halves:
        arrive_all(c_p[o])
        proj = jnp.concatenate([pr[o, j].astype(F32) for j in range(GROUPS)], axis=1)
        h1 = h_v[pl.ds(rows[o], HALF), :].astype(F32) + mod_v[2] * proj
        kept.append(h1)
        middle = layer_norm(h1) * (1.0 + mod_v[4]) + mod_v[3]
        x3[o, 0] = middle.astype(BF16)
        c_u.append(spread_tokens(x3, o))

    fresh_out[...] = kv[KEEP:, :]
    c_fw.wait()
    channels = fw_v.shape[0]
    spots = HALF * channels
    fw_tiled = jnp.concatenate([fw_v[...]] * HALF, axis=0)

    c_wu.wait()
    c_wd.wait()
    c_d = []
    own = []
    for o in halves:
        arrive_all(c_u[o])
        inner_v[...] = jax.nn.gelu(
            jnp.dot(x3[o].reshape(GROUPS * HALF, D), wu_v[...], preferred_element_type=F32),
            approximate=True,
        ).astype(BF16)
        part = jnp.dot(inner_v[...], wd_v[...], preferred_element_type=F32)
        own.append(part[0:HALF])
        parts[o] = part.astype(BF16).reshape(GROUPS, HALF, D)
        c_d.append(
            [remote(parts.at[o, slot], r4.at[o, i - 1], dev) for slot, dev, i in homeward]
        )

    outs = []
    for o in halves:
        arrive_all(c_d[o])
        total = own[o]
        for i in range(GROUPS - 1):
            total = total + r4[o, i].astype(F32)
        outs.append((kept[o] + mod_v[5] * total).astype(BF16))
        if o == 0:
            leave[...] = outs[0]
            c_a = remote(leave, arrive, other)

    c_fm.wait()
    c_nz.wait()
    c_tm.wait()
    c_gp.wait()
    c_a.wait_recv()
    arrived = arrive[...]
    next_out[...] = jnp.where(flip, outs[1], arrived)
    final_rows = jnp.where(flip, arrived, outs[1]).astype(F32)
    shifted = (layer_norm(final_rows) * (1.0 + fmod_v[1:2, :]) + fmod_v[0:1, :]).astype(BF16)
    each = dot_t(shifted, fw_tiled)
    row = lax.broadcasted_iota(jnp.int32, (HALF, spots), 0)
    col = lax.broadcasted_iota(jnp.int32, (HALF, spots), 1)
    noise = jnp.sum(jnp.where(lax.div(col, channels) == row, each, 0.0), axis=0, keepdims=True)
    now = jnp.full((1, spots), time_ref[0], jnp.int32)
    before = jnp.full((1, spots), time_ref[0] - gap_ref[0], jnp.int32)
    now_bar = alpha_bar(now.astype(F32))
    prev_bar = alpha_bar(before.astype(F32))
    clean = (noisy_v[...] - jnp.sqrt(1.0 - now_bar) * noise) / jnp.sqrt(now_bar)
    noise_out[...] = noise
    den_out[...] = jnp.sqrt(prev_bar) * clean + jnp.sqrt(1.0 - prev_bar) * noise

    for c in sends:
        c.wait_send()


def write_out(*refs):
    count = (len(refs) - 1) // 2
    sem = refs[-1]
    copies = [
        pltpu.make_async_copy(refs[i], refs[count + i], sem.at[i]) for i in range(count)
    ]
    for c in copies:
        c.start()
    for c in copies:
        c.wait()


def per_device(
    section_in,
    patch_index,
    stale_kv,
    modulation,
    final_mod,
    qkv_blocks,
    out_blocks,
    up_blocks,
    down_blocks,
    final_weight,
    noisy_latent,
    time_index,
    time_gap,
):
    any_spec = pl.BlockSpec(memory_space=pltpu.HBM)
    vmem = pl.BlockSpec(memory_space=pltpu.VMEM)
    spots = noisy_latent.shape[1]
    remote_count = 37
    outs = pl.pallas_call(
        kernel,
        name="relay_step",
        out_shape=(
            jax.ShapeDtypeStruct((TOK, 2 * D), BF16),
            jax.ShapeDtypeStruct((TOK // 2, D), BF16),
            jax.ShapeDtypeStruct((1, spots), F32),
            jax.ShapeDtypeStruct((1, spots), F32),
        ),
        in_specs=[any_spec] * 13,
        out_specs=(vmem,) * 4,
        scratch_shapes=[
            pltpu.SMEM((1, 1), jnp.int32),
            pltpu.SMEM((1,), jnp.int32),
            pltpu.SMEM((1,), jnp.int32),
            pltpu.VMEM((TOK, D), BF16),
            pltpu.VMEM((4 * TOK, 2 * D), BF16),
            pltpu.VMEM((6, 1, D), F32),
            pltpu.VMEM((2, D), F32),
            pltpu.VMEM((3 * BW, D), BF16),
            pltpu.VMEM((BW, D), BF16),
            pltpu.VMEM((D, D), BF16),
            pltpu.VMEM((D, D), BF16),
            pltpu.VMEM(final_weight.shape[::-1], BF16),
            pltpu.VMEM((1, spots), F32),
            pltpu.VMEM((2, GROUPS, HALF, D), BF16),
            pltpu.VMEM((2, GROUPS, HALF, 3 * BW), BF16),
            pltpu.VMEM((2, GROUPS, HALF, 3 * BW), BF16),
            pltpu.VMEM((KEEP + TOK, 2 * D), BF16),
            pltpu.VMEM((2, GROUPS, HALF, D), BF16),
            pltpu.VMEM((2, GROUPS, HALF, BW), BF16),
            pltpu.VMEM((2, GROUPS, HALF, BW), BF16),
            pltpu.VMEM((2, GROUPS, HALF, D), BF16),
            pltpu.VMEM((GROUPS * HALF, D), BF16),
            pltpu.VMEM((2, GROUPS, HALF, D), BF16),
            pltpu.VMEM((2, GROUPS - 1, HALF, D), BF16),
            pltpu.VMEM((HALF, D), BF16),
            pltpu.VMEM((HALF, D), BF16),
            pltpu.SemaphoreType.DMA((13,)),
            pltpu.SemaphoreType.DMA((remote_count,)),
            pltpu.SemaphoreType.DMA((remote_count,)),
        ],
        compiler_params=pltpu.CompilerParams(
            collective_id=0, has_side_effects=True, vmem_limit_bytes=48 * 1024 * 1024
        ),
    )(
        patch_index,
        time_index,
        time_gap,
        *(pltpu.with_memory_space_constraint(a, pltpu.HBM) for a in (        section_in[0, 0],
        stale_kv[0, 0],
        modulation[0, 0][:, None, :],
        final_mod[0],
        qkv_blocks[0, 0].T,
        out_blocks[0, 0].T,
        up_blocks[0, 0],
        down_blocks[0, 0],
        final_weight.T,
        noisy_latent,))
    )
    fresh, next_rows, noise_pred, denoised = pl.pallas_call(
        write_out,
        name="write_out",
        out_shape=tuple(jax.ShapeDtypeStruct(o.shape, o.dtype) for o in outs),
        in_specs=(vmem,) * 4,
        out_specs=(any_spec,) * 4,
        scratch_shapes=[pltpu.SemaphoreType.DMA((4,))],
    )(*(pltpu.with_memory_space_constraint(o, pltpu.VMEM) for o in outs))
    return (fresh[None, None], next_rows[None], noise_pred, denoised)


def solution(mesh):
    placed = (
        P("section", "req", None, None),
        P("section", "req"),
        P("section", "req", None, None),
        P("section", "req", None, None),
        P("req", None, None),
        P("section", "req", None, None),
        P("section", "req", None, None),
        P("section", "req", None, None),
        P("section", "req", None, None),
        P(),
        P("req", "section"),
        P("req"),
        P("req"),
    )
    return jax.shard_map(
        per_device,
        mesh=mesh,
        in_specs=placed,
        out_specs=(
            P("section", "req", None, None),
            P("req", "section", None),
            P("req", "section"),
            P("req", "section"),
        ),
        check_vma=False,
    )
```

```python
import functools

import jax
import jax.numpy as jnp
from jax import lax
from jax.experimental import pallas as pl
from jax.experimental.pallas import tpu as pltpu
from jax.sharding import PartitionSpec as P

MESH = pl.DeviceIdType.MESH
HEADS = 16
GROUPS = 4
NORM_EPS = 1e-06
BETA_LOW = 0.0001
BETA_HIGH = 0.02
TOK = 32
HALF = TOK // 2
D = 1152
BW = D // GROUPS
HEAD = D // HEADS
KEEP = 96
WIN = 384
RING = 8
QKV_CUTS = ((0, 512), (512, 3 * BW))
DOWN_CUTS = ((0, 512), (512, 1024), (1024, D))
F32 = jnp.float32
BF16 = jnp.bfloat16


def layer_norm(values):
    average = jnp.mean(values, axis=-1, keepdims=True)
    centred = values - average
    spread = jnp.mean(centred * centred, axis=-1, keepdims=True)
    return centred * lax.rsqrt(spread + NORM_EPS)


def dot(a, b):
    return jnp.dot(a, b, preferred_element_type=F32)


def dot_t(a, b):
    return lax.dot_general(a, b, (((1,), (1,)), ((), ())), preferred_element_type=F32)


def alpha_bar(moment):
    return jnp.exp(
        -(BETA_LOW * (moment + 1.0) + (BETA_HIGH - BETA_LOW) * moment * (moment + 1.0) / 1998.0)
    )


def kernel(
    patch_hbm,
    time_hbm,
    gap_hbm,
    h_hbm,
    stale_hbm,
    mod_hbm,
    fmod_hbm,
    wq_hbm,
    wo_hbm,
    wu_hbm,
    wd_hbm,
    fw_hbm,
    noisy_hbm,
    fresh_out,
    next_out,
    noise_out,
    den_out,
    patch_ref,
    time_ref,
    gap_ref,
    h_v,
    st_v,
    mod_v,
    fmod_v,
    wq_v,
    wo_v,
    wu_v,
    wd_v,
    fw_v,
    noisy_v,
    wqt,
    wot,
    fwt,
    sc,
    pb,
    x1,
    qs,
    qr,
    kv,
    x2,
    ps,
    pr,
    x3,
    inner_v,
    parts,
    r4,
    leave,
    arrive,
    lsem,
    ssem,
    rsem,
):
    s = lax.axis_index("section")
    r = lax.axis_index("req")
    z = lax.rem(r, RING)
    base = r - z
    odd = lax.rem(z, 2)
    mine = lax.rem(z, GROUPS)

    def at(dz):
        return (s, base + lax.rem(z + dz + RING, RING))

    far = 2 - 4 * odd
    outward = [(at(far), 3), (at(1), 2), (at(-1), 1)]
    homeward = [(3, at(-far), 3), (1, at(1), 2), (2, at(-1), 1)]
    other = (1 - s, r)
    rows = [pl.multiple_of(HALF * (1 - s), HALF), pl.multiple_of(HALF * s, HALF)]
    halves = (0, 1)

    local = []

    def load(i, src, dst):
        copy = pltpu.make_async_copy(src, dst, lsem.at[i])
        copy.start()
        local.append(copy)
        return copy

    c_h = load(0, h_hbm, h_v)
    c_mod = load(1, mod_hbm, mod_v)
    barrier = pltpu.get_barrier_semaphore()
    for peer in (at(1), at(-1), at(2), at(-2), other):
        pl.semaphore_signal(barrier, inc=1, device_id=peer, device_id_type=MESH)
    c_wq = load(3, wq_hbm, wq_v)
    c_pt = load(10, patch_hbm, patch_ref)
    c_st = load(2, stale_hbm, st_v)
    c_wo = load(4, wo_hbm, wo_v)
    c_wu = load(5, wu_hbm, wu_v)
    c_wd = load(6, wd_hbm, wd_v)
    c_fw = load(7, fw_hbm, fw_v)
    c_fm = load(8, fmod_hbm, fmod_v)
    c_nz = load(9, noisy_hbm, noisy_v)
    c_tm = load(11, time_hbm, time_ref)
    c_gp = load(12, gap_hbm, gap_ref)

    sends = []
    count = [0]

    def remote(src, dst, device):
        i = count[0]
        count[0] += 1
        copy = pltpu.make_async_remote_copy(
            src_ref=src,
            dst_ref=dst,
            send_sem=ssem.at[i],
            recv_sem=rsem.at[i],
            device_id=device,
            device_id_type=MESH,
        )
        copy.start()
        sends.append(copy)
        return copy

    def spread_tokens(buf, o):
        return [remote(buf.at[o, 0], buf.at[o, slot], dev) for dev, slot in outward]

    def arrive_all(copies):
        for c in copies:
            c.wait_recv()

    c_h.wait()
    c_mod.wait()
    normed = layer_norm(h_v[...].astype(F32)) * (1.0 + mod_v[1]) + mod_v[0]
    flip = s == 0
    x1[0, 0] = jnp.where(flip, normed[HALF:], normed[:HALF]).astype(BF16)
    x1[1, 0] = jnp.where(flip, normed[:HALF], normed[HALF:]).astype(BF16)

    pl.semaphore_wait(barrier, 5)
    c_x = [spread_tokens(x1, o) for o in halves]

    c_st.wait()
    c_pt.wait()
    patch = patch_ref[0, 0]
    for k in range(3):
        low = st_v[k * TOK : (k + 1) * TOK, :]
        high = st_v[(k + 1) * TOK : (k + 2) * TOK, :]
        kv[k * TOK : (k + 1) * TOK, :] = jnp.where(patch <= k, high, low)

    c_wq.wait()
    for c in range(0, D, 128):
        wqt[c : c + 128, :] = wq_v[:, c : c + 128].T
    c_q = []
    for o in halves:
        arrive_all(c_x[o])
        c_q.append([])
        for a, b in QKV_CUTS:
            qkv = dot(x1[o].reshape(GROUPS * HALF, D), wqt[:, a:b]).astype(BF16)
            qs[o, :, :, a:b] = qkv.reshape(GROUPS, HALF, b - a)
            c_q[o] += [
                remote(qs.at[o, slot, :, a:b], qr.at[o, mine, :, a:b], dev)
                for slot, dev, _ in homeward
            ]
            qr[o, mine, :, a:b] = qkv[0:HALF]

    c_wo.wait()
    for c in range(0, D, 128):
        wot[c : c + 128, :] = wo_v[:, c : c + 128].T
    c_fw.wait()
    channels = fw_v.shape[0]
    spots = HALF * channels
    fwt[...] = jnp.concatenate([fw_v[...]] * HALF, axis=0).T

    queries = []
    for o in halves:
        arrive_all(c_q[o])
        blocks = [qr[o, j].astype(F32) for j in range(GROUPS)]
        queries.append(jnp.concatenate([b[:, 0:BW] for b in blocks], axis=1))
        fresh = jnp.concatenate(
            [b[:, BW : 2 * BW] for b in blocks] + [b[:, 2 * BW :] for b in blocks], axis=1
        )
        kv[pl.ds(KEEP + rows[o], HALF), :] = fresh.astype(BF16)

    lane = lax.broadcasted_iota(jnp.int32, (HALF, WIN), 1)

    def heads_of(j):
        starts = [TOK * j + a * HEAD for a in range(HEADS // GROUPS)]
        return [(lane >= low) & (lane < low + HEAD) for low in starts]

    block = (HEADS // GROUPS) * HALF
    c_m = []
    for o in halves:
        for j in range(GROUPS):
            q = queries[o][:, 256 * j : 256 * j + WIN]
            spread = jnp.concatenate([jnp.where(m, q, 0.0) for m in heads_of(j)], axis=0)
            sc[j * block : (j + 1) * block, :] = dot_t(
                spread.astype(BF16), kv[:, 256 * j : 256 * j + WIN]
            ) * HEAD ** (-0.5)
        scores = sc[...]
        raised = jnp.exp(scores - jnp.max(scores, axis=-1, keepdims=True))
        pb[...] = (raised / jnp.sum(raised, axis=-1, keepdims=True)).astype(BF16)
        wins = []
        for j in range(GROUPS):
            mixed = dot(
                pb[j * block : (j + 1) * block, :], kv[:, D + 256 * j : D + 256 * j + WIN]
            )
            picked = jnp.zeros((HALF, WIN), F32)
            for a, m in enumerate(heads_of(j)):
                picked = jnp.where(m, mixed[a * HALF : (a + 1) * HALF], picked)
            wins.append(picked)
        cuts = [wins[0][:, 0:256]]
        for j in range(1, GROUPS):
            cuts.append(wins[j - 1][:, 256:WIN] + wins[j][:, 0:128])
            cuts.append(wins[j][:, 128:256])
        cuts.append(wins[GROUPS - 1][:, 256:WIN])
        x2[o, 0] = jnp.concatenate(cuts, axis=1).astype(BF16)
        c_m.append(spread_tokens(x2, o))

    c_p = []
    for o in halves:
        arrive_all(c_m[o])
        proj = dot(x2[o].reshape(GROUPS * HALF, D), wot[...]).astype(BF16)
        ps[o] = proj.reshape(GROUPS, HALF, BW)
        c_p.append([remote(ps.at[o, slot], pr.at[o, mine], dev) for slot, dev, _ in homeward])
        pr[o, mine] = proj[0:HALF]

    c_u = []
    kept = []
    for o in halves:
        arrive_all(c_p[o])
        proj = jnp.concatenate([pr[o, j].astype(F32) for j in range(GROUPS)], axis=1)
        h1 = h_v[pl.ds(rows[o], HALF), :].astype(F32) + mod_v[2] * proj
        kept.append(h1)
        middle = layer_norm(h1) * (1.0 + mod_v[4]) + mod_v[3]
        x3[o, 0] = middle.astype(BF16)
        c_u.append(spread_tokens(x3, o))

    fresh_out[...] = kv[KEEP:, :]
    c_wu.wait()
    c_wd.wait()
    c_d = []
    own = []
    for o in halves:
        arrive_all(c_u[o])
        inner_v[...] = jax.nn.gelu(
            dot(x3[o].reshape(GROUPS * HALF, D), wu_v[...]), approximate=True
        ).astype(BF16)
        own.append([])
        c_d.append([])
        for a, b in DOWN_CUTS:
            part = dot(inner_v[...], wd_v[:, a:b])
            own[o].append(part[0:HALF])
            parts[o, :, :, a:b] = part.astype(BF16).reshape(GROUPS, HALF, b - a)
            c_d[o] += [
                remote(parts.at[o, slot, :, a:b], r4.at[o, i - 1, :, a:b], dev)
                for slot, dev, i in homeward
            ]

    c_tm.wait()
    c_gp.wait()
    now = jnp.full((1, spots), time_ref[0], jnp.int32)
    before = jnp.full((1, spots), time_ref[0] - gap_ref[0], jnp.int32)
    now_bar = alpha_bar(now.astype(F32))
    prev_bar = alpha_bar(before.astype(F32))
    now_noise = jnp.sqrt(1.0 - now_bar)
    now_root = jnp.sqrt(now_bar)
    prev_noise = jnp.sqrt(1.0 - prev_bar)
    prev_root = jnp.sqrt(prev_bar)
    row = lax.broadcasted_iota(jnp.int32, (HALF, spots), 0)
    col = lax.broadcasted_iota(jnp.int32, (HALF, spots), 1)
    token = lax.div(col, channels) == row
    c_fm.wait()
    c_nz.wait()

    outs = []
    for o in halves:
        arrive_all(c_d[o])
        total = jnp.concatenate(own[o], axis=1)
        for i in range(GROUPS - 1):
            total = total + r4[o, i].astype(F32)
        outs.append((kept[o] + mod_v[5] * total).astype(BF16))
        if o == 0:
            leave[...] = outs[0]
            c_a = remote(leave, arrive, other)

    c_a.wait_recv()
    arrived = arrive[...]
    next_out[...] = jnp.where(flip, outs[1], arrived)
    final_rows = jnp.where(flip, arrived, outs[1]).astype(F32)
    shifted = (layer_norm(final_rows) * (1.0 + fmod_v[1:2, :]) + fmod_v[0:1, :]).astype(BF16)
    each = dot(shifted, fwt[...])
    noise = jnp.sum(jnp.where(token, each, 0.0), axis=0, keepdims=True)
    clean = (noisy_v[...] - now_noise * noise) / now_root
    noise_out[...] = noise
    den_out[...] = prev_root * clean + prev_noise * noise

    for c in sends:
        c.wait_send()


def write_out(*refs):
    count = (len(refs) - 1) // 2
    sem = refs[-1]
    copies = [
        pltpu.make_async_copy(refs[i], refs[count + i], sem.at[i]) for i in range(count)
    ]
    for c in copies:
        c.start()
    for c in copies:
        c.wait()


def per_device(
    section_in,
    patch_index,
    stale_kv,
    modulation,
    final_mod,
    qkv_blocks,
    out_blocks,
    up_blocks,
    down_blocks,
    final_weight,
    noisy_latent,
    time_index,
    time_gap,
):
    any_spec = pl.BlockSpec(memory_space=pltpu.HBM)
    vmem = pl.BlockSpec(memory_space=pltpu.VMEM)
    spots = noisy_latent.shape[1]
    remote_count = 55
    outs = pl.pallas_call(
        kernel,
        name="relay_step",
        out_shape=(
            jax.ShapeDtypeStruct((TOK, 2 * D), BF16),
            jax.ShapeDtypeStruct((TOK // 2, D), BF16),
            jax.ShapeDtypeStruct((1, spots), F32),
            jax.ShapeDtypeStruct((1, spots), F32),
        ),
        in_specs=[any_spec] * 13,
        out_specs=(vmem,) * 4,
        scratch_shapes=[
            pltpu.SMEM((1, 1), jnp.int32),
            pltpu.SMEM((1,), jnp.int32),
            pltpu.SMEM((1,), jnp.int32),
            pltpu.VMEM((TOK, D), BF16),
            pltpu.VMEM((4 * TOK, 2 * D), BF16),
            pltpu.VMEM((6, 1, D), F32),
            pltpu.VMEM((2, D), F32),
            pltpu.VMEM((3 * BW, D), BF16),
            pltpu.VMEM((BW, D), BF16),
            pltpu.VMEM((D, D), BF16),
            pltpu.VMEM((D, D), BF16),
            pltpu.VMEM(final_weight.shape[::-1], BF16),
            pltpu.VMEM((1, spots), F32),
            pltpu.VMEM((D, 3 * BW), BF16),
            pltpu.VMEM((D, BW), BF16),
            pltpu.VMEM((D, spots), BF16),
            pltpu.VMEM((HEADS * HALF, KEEP + TOK), F32),
            pltpu.VMEM((HEADS * HALF, KEEP + TOK), BF16),
            pltpu.VMEM((2, GROUPS, HALF, D), BF16),
            pltpu.VMEM((2, GROUPS, HALF, 3 * BW), BF16),
            pltpu.VMEM((2, GROUPS, HALF, 3 * BW), BF16),
            pltpu.VMEM((KEEP + TOK, 2 * D), BF16),
            pltpu.VMEM((2, GROUPS, HALF, D), BF16),
            pltpu.VMEM((2, GROUPS, HALF, BW), BF16),
            pltpu.VMEM((2, GROUPS, HALF, BW), BF16),
            pltpu.VMEM((2, GROUPS, HALF, D), BF16),
            pltpu.VMEM((GROUPS * HALF, D), BF16),
            pltpu.VMEM((2, GROUPS, HALF, D), BF16),
            pltpu.VMEM((2, GROUPS - 1, HALF, D), BF16),
            pltpu.VMEM((HALF, D), BF16),
            pltpu.VMEM((HALF, D), BF16),
            pltpu.SemaphoreType.DMA((13,)),
            pltpu.SemaphoreType.DMA((remote_count,)),
            pltpu.SemaphoreType.DMA((remote_count,)),
        ],
        compiler_params=pltpu.CompilerParams(
            collective_id=0, has_side_effects=True, vmem_limit_bytes=48 * 1024 * 1024
        ),
    )(
        patch_index,
        time_index,
        time_gap,
        *(pltpu.with_memory_space_constraint(a, pltpu.HBM) for a in (        section_in[0, 0],
        stale_kv[0, 0],
        modulation[0, 0][:, None, :],
        final_mod[0],
        qkv_blocks[0, 0].T,
        out_blocks[0, 0].T,
        up_blocks[0, 0],
        down_blocks[0, 0],
        final_weight.T,
        noisy_latent,))
    )
    fresh, next_rows, noise_pred, denoised = pl.pallas_call(
        write_out,
        name="write_out",
        out_shape=tuple(jax.ShapeDtypeStruct(o.shape, o.dtype) for o in outs),
        in_specs=(vmem,) * 4,
        out_specs=(any_spec,) * 4,
        scratch_shapes=[pltpu.SemaphoreType.DMA((4,))],
    )(*(pltpu.with_memory_space_constraint(o, pltpu.VMEM) for o in outs))
    return (fresh[None, None], next_rows[None], noise_pred, denoised)


def solution(mesh):
    placed = (
        P("section", "req", None, None),
        P("section", "req"),
        P("section", "req", None, None),
        P("section", "req", None, None),
        P("req", None, None),
        P("section", "req", None, None),
        P("section", "req", None, None),
        P("section", "req", None, None),
        P("section", "req", None, None),
        P(),
        P("req", "section"),
        P("req"),
        P("req"),
    )
    return jax.shard_map(
        per_device,
        mesh=mesh,
        in_specs=placed,
        out_specs=(
            P("section", "req", None, None),
            P("req", "section", None),
            P("req", "section"),
            P("req", "section"),
        ),
        check_vma=False,
    )
```

```python
import functools

import jax
import jax.numpy as jnp
from jax import lax
from jax.experimental import pallas as pl
from jax.experimental.pallas import tpu as pltpu
from jax.sharding import PartitionSpec as P

MESH = pl.DeviceIdType.MESH
HEADS = 16
GROUPS = 4
NORM_EPS = 1e-06
BETA_LOW = 0.0001
BETA_HIGH = 0.02
TOK = 32
HALF = TOK // 2
D = 1152
BW = D // GROUPS
HEAD = D // HEADS
KEEP = 96
WIN = 384
RING = 8
QKV_CUTS = ((0, 512), (512, 3 * BW))
DOWN_CUTS = ((0, 512), (512, 1024), (1024, D))
F32 = jnp.float32
BF16 = jnp.bfloat16


def layer_norm(values):
    average = jnp.mean(values, axis=-1, keepdims=True)
    centred = values - average
    spread = jnp.mean(centred * centred, axis=-1, keepdims=True)
    return centred * lax.rsqrt(spread + NORM_EPS)


def dot(a, b):
    return jnp.dot(a, b, preferred_element_type=F32)


def dot_t(a, b):
    return lax.dot_general(a, b, (((1,), (1,)), ((), ())), preferred_element_type=F32)


def alpha_bar(moment):
    return jnp.exp(
        -(BETA_LOW * (moment + 1.0) + (BETA_HIGH - BETA_LOW) * moment * (moment + 1.0) / 1998.0)
    )


def kernel(
    patch_hbm,
    time_hbm,
    gap_hbm,
    h_hbm,
    stale_hbm,
    mod_hbm,
    fmod_hbm,
    wq_hbm,
    wo_hbm,
    wu_hbm,
    wd_hbm,
    fw_hbm,
    noisy_hbm,
    fresh_out,
    next_out,
    noise_out,
    den_out,
    patch_ref,
    time_ref,
    gap_ref,
    h_v,
    st_v,
    mod_v,
    fmod_v,
    wq_v,
    wo_v,
    wu_v,
    wd_v,
    fw_v,
    noisy_v,
    wqt,
    wot,
    fwt,
    sc,
    pb,
    x1,
    qs,
    qr,
    kv,
    x2,
    ps,
    pr,
    x3,
    inner_v,
    parts,
    r4,
    rx,
    leave,
    arrive,
    gate,
    lsem,
    ssem,
    rsem,
):
    s = lax.axis_index("section")
    r = lax.axis_index("req")
    z = lax.rem(r, RING)
    base = r - z
    odd = lax.rem(z, 2)
    mine = lax.rem(z, GROUPS)

    def at(dz, section=s):
        return (section, base + lax.rem(z + dz + RING, RING))

    swap = 2 - 4 * lax.rem(lax.div(z, 2), 2)
    skip = 2 - 4 * odd
    far_to = (swap, skip)
    far_from = (swap, -skip)
    outward = [[(at(far), 3), (at(1), 2), (at(-1), 1)] for far in far_to]
    homeward = [[(3, at(far), 3), (1, at(1), 2), (2, at(-1), 1)] for far in far_from]
    across = 1 - s
    other = (across, r)
    crossing = [(3, at(far_from[0], across), 3), (1, at(1, across), 2), (2, at(-1, across), 1)]
    rows = [pl.multiple_of(HALF * (1 - s), HALF), pl.multiple_of(HALF * s, HALF)]
    halves = (0, 1)

    local = []

    def load(i, src, dst):
        copy = pltpu.make_async_copy(src, dst, lsem.at[i])
        copy.start()
        local.append(copy)
        return copy

    barrier = pltpu.get_barrier_semaphore()
    steps = (2, -2, 1, -1)
    peers = [at(dz) for dz in steps] + [at(dz, across) for dz in steps] + [other]
    for peer in peers:
        pl.semaphore_signal(barrier, inc=1, device_id=peer, device_id_type=MESH)
    c_h = load(0, h_hbm, h_v)
    c_mod = load(1, mod_hbm, mod_v)
    c_wq = load(3, wq_hbm, wq_v)
    c_pt = load(10, patch_hbm, patch_ref)
    c_st = load(2, stale_hbm, st_v)
    c_wo = load(4, wo_hbm, wo_v)
    c_wu = load(5, wu_hbm, wu_v)
    c_wd = load(6, wd_hbm, wd_v)
    c_fw = load(7, fw_hbm, fw_v)
    c_fm = load(8, fmod_hbm, fmod_v)
    c_nz = load(9, noisy_hbm, noisy_v)
    c_tm = load(11, time_hbm, time_ref)
    c_gp = load(12, gap_hbm, gap_ref)

    sends = []
    count = [0]

    def remote(src, dst, device):
        i = count[0]
        count[0] += 1
        copy = pltpu.make_async_remote_copy(
            src_ref=src,
            dst_ref=dst,
            send_sem=ssem.at[i],
            recv_sem=rsem.at[i],
            device_id=device,
            device_id_type=MESH,
        )
        copy.start()
        sends.append(copy)
        return copy

    def spread_tokens(buf, o):
        return [remote(buf.at[o, 0], buf.at[o, slot], dev) for dev, slot in outward[o]]

    def arrive_all(copies):
        for c in copies:
            c.wait_recv()

    c_h.wait()
    c_mod.wait()
    normed = layer_norm(h_v[...].astype(F32)) * (1.0 + mod_v[1]) + mod_v[0]
    flip = s == 0
    x1[0, 0] = jnp.where(flip, normed[HALF:], normed[:HALF]).astype(BF16)
    x1[1, 0] = jnp.where(flip, normed[:HALF], normed[HALF:]).astype(BF16)

    pl.semaphore_wait(barrier, len(peers))
    c_x = [spread_tokens(x1, o) for o in halves]

    c_st.wait()
    c_pt.wait()
    patch = patch_ref[0, 0]
    for k in range(3):
        low = st_v[k * TOK : (k + 1) * TOK, :]
        high = st_v[(k + 1) * TOK : (k + 2) * TOK, :]
        kv[k * TOK : (k + 1) * TOK, :] = jnp.where(patch <= k, high, low)

    c_wq.wait()
    for c in range(0, D, 128):
        wqt[c : c + 128, :] = wq_v[:, c : c + 128].T
    c_q = []
    for o in halves:
        arrive_all(c_x[o])
        c_q.append([])
        for a, b in QKV_CUTS:
            qkv = dot(x1[o].reshape(GROUPS * HALF, D), wqt[:, a:b]).astype(BF16)
            qs[o, :, :, a:b] = qkv.reshape(GROUPS, HALF, b - a)
            c_q[o] += [
                remote(qs.at[o, slot, :, a:b], qr.at[o, mine, :, a:b], dev)
                for slot, dev, _ in homeward[o]
            ]
            qr[o, mine, :, a:b] = qkv[0:HALF]

    c_wo.wait()
    for c in range(0, D, 128):
        wot[c : c + 128, :] = wo_v[:, c : c + 128].T
    c_fw.wait()
    channels = fw_v.shape[0]
    spots = HALF * channels
    fwt[...] = jnp.concatenate([fw_v[...]] * HALF, axis=0).T

    queries = []
    for o in halves:
        arrive_all(c_q[o])
        blocks = [qr[o, j].astype(F32) for j in range(GROUPS)]
        queries.append(jnp.concatenate([b[:, 0:BW] for b in blocks], axis=1))
        fresh = jnp.concatenate(
            [b[:, BW : 2 * BW] for b in blocks] + [b[:, 2 * BW :] for b in blocks], axis=1
        )
        kv[pl.ds(KEEP + rows[o], HALF), :] = fresh.astype(BF16)

    lane = lax.broadcasted_iota(jnp.int32, (TOK, WIN), 1)

    def heads_of(j):
        starts = [TOK * j + a * HEAD for a in range(HEADS // GROUPS)]
        return [(lane >= low) & (lane < low + HEAD) for low in starts]

    block = (HEADS // GROUPS) * TOK
    query = jnp.concatenate(queries, axis=0)
    for j in range(GROUPS):
        q = query[:, 256 * j : 256 * j + WIN]
        spread = jnp.concatenate([jnp.where(m, q, 0.0) for m in heads_of(j)], axis=0)
        sc[j * block : (j + 1) * block, :] = dot_t(
            spread.astype(BF16), kv[:, 256 * j : 256 * j + WIN]
        ) * HEAD ** (-0.5)
    scores = sc[...]
    raised = jnp.exp(scores - jnp.max(scores, axis=-1, keepdims=True))
    pb[...] = (raised / jnp.sum(raised, axis=-1, keepdims=True)).astype(BF16)
    wins = []
    for j in range(GROUPS):
        mixed = dot(pb[j * block : (j + 1) * block, :], kv[:, D + 256 * j : D + 256 * j + WIN])
        picked = jnp.zeros((TOK, WIN), F32)
        for a, m in enumerate(heads_of(j)):
            picked = jnp.where(m, mixed[a * TOK : (a + 1) * TOK], picked)
        wins.append(picked)
    cuts = [wins[0][:, 0:256]]
    for j in range(1, GROUPS):
        cuts.append(wins[j - 1][:, 256:WIN] + wins[j][:, 0:128])
        cuts.append(wins[j][:, 128:256])
    cuts.append(wins[GROUPS - 1][:, 256:WIN])
    whole = jnp.concatenate(cuts, axis=1).astype(BF16)
    c_m = []
    for o in halves:
        x2[o, 0] = whole[o * HALF : (o + 1) * HALF]
        c_m.append(spread_tokens(x2, o))

    c_p = []
    for o in halves:
        arrive_all(c_m[o])
        proj = dot(x2[o].reshape(GROUPS * HALF, D), wot[...]).astype(BF16)
        ps[o] = proj.reshape(GROUPS, HALF, BW)
        c_p.append([remote(ps.at[o, slot], pr.at[o, mine], dev) for slot, dev, _ in homeward[o]])
        pr[o, mine] = proj[0:HALF]

    c_u = []
    kept = []
    for o in halves:
        arrive_all(c_p[o])
        proj = jnp.concatenate([pr[o, j].astype(F32) for j in range(GROUPS)], axis=1)
        h1 = h_v[pl.ds(rows[o], HALF), :].astype(F32) + mod_v[2] * proj
        kept.append(h1)
        middle = layer_norm(h1) * (1.0 + mod_v[4]) + mod_v[3]
        x3[o, 0] = middle.astype(BF16)
        c_u.append(spread_tokens(x3, o))
        if o == 0:
            leave[...] = h1
            c_l = [remote(leave, arrive, other), remote(mod_v.at[5], gate, other)]

    fresh_out[...] = kv[KEEP:, :]
    c_wu.wait()
    c_wd.wait()
    early = list(sends)
    c_d = []
    for o in halves:
        arrive_all(c_u[o])
        inner_v[...] = jax.nn.gelu(
            dot(x3[o].reshape(GROUPS * HALF, D), wu_v[...]), approximate=True
        ).astype(BF16)
        own = []
        c_d.append([])
        for a, b in DOWN_CUTS:
            part = dot(inner_v[...], wd_v[:, a:b])
            own.append(part[0:HALF])
            parts[o, :, :, a:b] = part.astype(BF16).reshape(GROUPS, HALF, b - a)
            routes = crossing + [(0, other, GROUPS)] if o == 0 else homeward[o]
            into = rx if o == 0 else r4
            c_d[o] += [
                remote(parts.at[o, slot, :, a:b], into.at[i - 1, :, a:b], dev)
                for slot, dev, i in routes
            ]

    c_tm.wait()
    c_gp.wait()
    now = jnp.full((1, spots), time_ref[0], jnp.int32)
    before = jnp.full((1, spots), time_ref[0] - gap_ref[0], jnp.int32)
    now_bar = alpha_bar(now.astype(F32))
    prev_bar = alpha_bar(before.astype(F32))
    now_noise = jnp.sqrt(1.0 - now_bar)
    now_root = jnp.sqrt(now_bar)
    prev_noise = jnp.sqrt(1.0 - prev_bar)
    prev_root = jnp.sqrt(prev_bar)
    row = lax.broadcasted_iota(jnp.int32, (HALF, spots), 0)
    col = lax.broadcasted_iota(jnp.int32, (HALF, spots), 1)
    token = lax.div(col, channels) == row
    c_fm.wait()
    c_nz.wait()
    for c in early:
        c.wait_send()

    arrive_all(c_l)
    arrive_all(c_d[0])
    total = rx[0].astype(F32)
    for i in range(1, GROUPS):
        total = total + rx[i].astype(F32)
    out_across = arrive[...] + gate[...] * total
    for c in c_d[0]:
        c.wait_send()

    arrive_all(c_d[1])
    total = jnp.concatenate(own, axis=1)
    for i in range(GROUPS - 1):
        total = total + r4[i].astype(F32)
    out_here = kept[1] + mod_v[5] * total
    next_out[...] = jnp.where(flip, out_here, out_across).astype(BF16)
    final_rows = jnp.where(flip, out_across, out_here).astype(BF16).astype(F32)
    shifted = (layer_norm(final_rows) * (1.0 + fmod_v[1:2, :]) + fmod_v[0:1, :]).astype(BF16)
    each = dot(shifted, fwt[...])
    noise = jnp.sum(jnp.where(token, each, 0.0), axis=0, keepdims=True)
    clean = (noisy_v[...] - now_noise * noise) / now_root
    noise_out[...] = noise
    den_out[...] = prev_root * clean + prev_noise * noise

    for c in c_d[1]:
        c.wait_send()


def write_out(*refs):
    count = (len(refs) - 1) // 2
    sem = refs[-1]
    copies = [
        pltpu.make_async_copy(refs[i], refs[count + i], sem.at[i]) for i in range(count)
    ]
    for c in copies:
        c.start()
    for c in copies:
        c.wait()


def per_device(
    section_in,
    patch_index,
    stale_kv,
    modulation,
    final_mod,
    qkv_blocks,
    out_blocks,
    up_blocks,
    down_blocks,
    final_weight,
    noisy_latent,
    time_index,
    time_gap,
):
    any_spec = pl.BlockSpec(memory_space=pltpu.HBM)
    vmem = pl.BlockSpec(memory_space=pltpu.VMEM)
    spots = noisy_latent.shape[1]
    remote_count = 59
    outs = pl.pallas_call(
        kernel,
        name="relay_step",
        out_shape=(
            jax.ShapeDtypeStruct((TOK, 2 * D), BF16),
            jax.ShapeDtypeStruct((TOK // 2, D), BF16),
            jax.ShapeDtypeStruct((1, spots), F32),
            jax.ShapeDtypeStruct((1, spots), F32),
        ),
        in_specs=[any_spec] * 13,
        out_specs=(vmem,) * 4,
        scratch_shapes=[
            pltpu.SMEM((1, 1), jnp.int32),
            pltpu.SMEM((1,), jnp.int32),
            pltpu.SMEM((1,), jnp.int32),
            pltpu.VMEM((TOK, D), BF16),
            pltpu.VMEM((4 * TOK, 2 * D), BF16),
            pltpu.VMEM((6, 1, D), F32),
            pltpu.VMEM((2, D), F32),
            pltpu.VMEM((3 * BW, D), BF16),
            pltpu.VMEM((BW, D), BF16),
            pltpu.VMEM((D, D), BF16),
            pltpu.VMEM((D, D), BF16),
            pltpu.VMEM(final_weight.shape[::-1], BF16),
            pltpu.VMEM((1, spots), F32),
            pltpu.VMEM((D, 3 * BW), BF16),
            pltpu.VMEM((D, BW), BF16),
            pltpu.VMEM((D, spots), BF16),
            pltpu.VMEM((HEADS * TOK, KEEP + TOK), F32),
            pltpu.VMEM((HEADS * TOK, KEEP + TOK), BF16),
            pltpu.VMEM((2, GROUPS, HALF, D), BF16),
            pltpu.VMEM((2, GROUPS, HALF, 3 * BW), BF16),
            pltpu.VMEM((2, GROUPS, HALF, 3 * BW), BF16),
            pltpu.VMEM((KEEP + TOK, 2 * D), BF16),
            pltpu.VMEM((2, GROUPS, HALF, D), BF16),
            pltpu.VMEM((2, GROUPS, HALF, BW), BF16),
            pltpu.VMEM((2, GROUPS, HALF, BW), BF16),
            pltpu.VMEM((2, GROUPS, HALF, D), BF16),
            pltpu.VMEM((GROUPS * HALF, D), BF16),
            pltpu.VMEM((2, GROUPS, HALF, D), BF16),
            pltpu.VMEM((GROUPS - 1, HALF, D), BF16),
            pltpu.VMEM((GROUPS, HALF, D), BF16),
            pltpu.VMEM((HALF, D), F32),
            pltpu.VMEM((HALF, D), F32),
            pltpu.VMEM((1, D), F32),
            pltpu.SemaphoreType.DMA((13,)),
            pltpu.SemaphoreType.DMA((remote_count,)),
            pltpu.SemaphoreType.DMA((remote_count,)),
        ],
        compiler_params=pltpu.CompilerParams(
            collective_id=0, has_side_effects=True, vmem_limit_bytes=48 * 1024 * 1024
        ),
    )(
        patch_index,
        time_index,
        time_gap,
        *(pltpu.with_memory_space_constraint(a, pltpu.HBM) for a in (        section_in[0, 0],
        stale_kv[0, 0],
        modulation[0, 0][:, None, :],
        final_mod[0],
        qkv_blocks[0, 0].T,
        out_blocks[0, 0].T,
        up_blocks[0, 0],
        down_blocks[0, 0],
        final_weight.T,
        noisy_latent,))
    )
    fresh, next_rows, noise_pred, denoised = pl.pallas_call(
        write_out,
        name="write_out",
        out_shape=tuple(jax.ShapeDtypeStruct(o.shape, o.dtype) for o in outs),
        in_specs=(vmem,) * 4,
        out_specs=(any_spec,) * 4,
        scratch_shapes=[pltpu.SemaphoreType.DMA((4,))],
    )(*(pltpu.with_memory_space_constraint(o, pltpu.VMEM) for o in outs))
    return (fresh[None, None], next_rows[None], noise_pred, denoised)


def solution(mesh):
    placed = (
        P("section", "req", None, None),
        P("section", "req"),
        P("section", "req", None, None),
        P("section", "req", None, None),
        P("req", None, None),
        P("section", "req", None, None),
        P("section", "req", None, None),
        P("section", "req", None, None),
        P("section", "req", None, None),
        P(),
        P("req", "section"),
        P("req"),
        P("req"),
    )
    return jax.shard_map(
        per_device,
        mesh=mesh,
        in_specs=placed,
        out_specs=(
            P("section", "req", None, None),
            P("req", "section", None),
            P("req", "section"),
            P("req", "section"),
        ),
        check_vma=False,
    )
```

```python
import functools

import jax
import jax.numpy as jnp
from jax import lax
from jax.experimental import pallas as pl
from jax.experimental.pallas import tpu as pltpu
from jax.sharding import PartitionSpec as P

MESH = pl.DeviceIdType.MESH
HEADS = 16
GROUPS = 4
NORM_EPS = 1e-06
BETA_LOW = 0.0001
BETA_HIGH = 0.02
TOK = 32
HALF = TOK // 2
D = 1152
BW = D // GROUPS
HEAD = D // HEADS
KEEP = 96
WIN = 384
RING = 8
QKV_CUTS = ((0, 3 * BW),)
DOWN_CUTS = ((0, 768), (768, D))
F32 = jnp.float32
BF16 = jnp.bfloat16


def layer_norm(values):
    average = jnp.mean(values, axis=-1, keepdims=True)
    centred = values - average
    spread = jnp.mean(centred * centred, axis=-1, keepdims=True)
    return centred * lax.rsqrt(spread + NORM_EPS)


def dot(a, b):
    return jnp.dot(a, b, preferred_element_type=F32)


def dot_t(a, b):
    return lax.dot_general(a, b, (((1,), (1,)), ((), ())), preferred_element_type=F32)


def alpha_bar(moment):
    return jnp.exp(
        -(BETA_LOW * (moment + 1.0) + (BETA_HIGH - BETA_LOW) * moment * (moment + 1.0) / 1998.0)
    )


def kernel(
    patch_hbm,
    time_hbm,
    gap_hbm,
    h_hbm,
    stale_hbm,
    mod_hbm,
    fmod_hbm,
    wq_hbm,
    wo_hbm,
    wu_hbm,
    wd_hbm,
    fw_hbm,
    noisy_hbm,
    fresh_out,
    next_out,
    noise_out,
    den_out,
    patch_ref,
    time_ref,
    gap_ref,
    h_v,
    st_v,
    mod_v,
    fmod_v,
    wq_v,
    wo_v,
    wu_v,
    wd_v,
    fw_v,
    noisy_v,
    wqt,
    wot,
    fwt,
    sc,
    pb,
    x1,
    qs,
    qr,
    kv,
    x2,
    ps,
    pr,
    x3,
    inner_v,
    parts,
    r4,
    rx,
    leave,
    arrive,
    gate,
    lsem,
    ssem,
    rsem,
):
    s = lax.axis_index("section")
    r = lax.axis_index("req")
    z = lax.rem(r, RING)
    base = r - z
    odd = lax.rem(z, 2)
    mine = lax.rem(z, GROUPS)

    def at(dz, section=s):
        return (section, base + lax.rem(z + dz + RING, RING))

    swap = 2 - 4 * lax.rem(lax.div(z, 2), 2)
    skip = 2 - 4 * odd
    far_to = (swap, skip)
    far_from = (swap, -skip)
    outward = [[(at(far), 3), (at(1), 2), (at(-1), 1)] for far in far_to]
    homeward = [[(3, at(far), 3), (1, at(1), 2), (2, at(-1), 1)] for far in far_from]
    across = 1 - s
    other = (across, r)
    crossing = [(3, at(far_from[0], across), 3), (1, at(1, across), 2), (2, at(-1, across), 1)]
    rows = [pl.multiple_of(HALF * (1 - s), HALF), pl.multiple_of(HALF * s, HALF)]
    halves = (0, 1)

    local = []

    def load(i, src, dst):
        copy = pltpu.make_async_copy(src, dst, lsem.at[i])
        copy.start()
        local.append(copy)
        return copy

    barrier = pltpu.get_barrier_semaphore()
    steps = (2, -2, 1, -1)
    peers = [at(dz) for dz in steps] + [at(dz, across) for dz in steps] + [other]
    for peer in peers:
        pl.semaphore_signal(barrier, inc=1, device_id=peer, device_id_type=MESH)
    c_h = load(0, h_hbm, h_v)
    c_mod = load(1, mod_hbm, mod_v)
    c_wq = load(3, wq_hbm, wq_v)
    c_pt = load(10, patch_hbm, patch_ref)
    c_st = load(2, stale_hbm, st_v)
    c_wo = load(4, wo_hbm, wo_v)
    c_wu = load(5, wu_hbm, wu_v)
    c_wd = load(6, wd_hbm, wd_v)
    c_fw = load(7, fw_hbm, fw_v)
    c_fm = load(8, fmod_hbm, fmod_v)
    c_nz = load(9, noisy_hbm, noisy_v)
    c_tm = load(11, time_hbm, time_ref)
    c_gp = load(12, gap_hbm, gap_ref)

    sends = []
    count = [0]

    def remote(src, dst, device):
        i = count[0]
        count[0] += 1
        copy = pltpu.make_async_remote_copy(
            src_ref=src,
            dst_ref=dst,
            send_sem=ssem.at[i],
            recv_sem=rsem.at[i],
            device_id=device,
            device_id_type=MESH,
        )
        copy.start()
        sends.append(copy)
        return copy

    def spread_tokens(buf, o):
        return [remote(buf.at[o, 0], buf.at[o, slot], dev) for dev, slot in outward[o]]

    def arrive_all(copies):
        for c in copies:
            c.wait_recv()

    c_h.wait()
    c_mod.wait()
    normed = layer_norm(h_v[...].astype(F32)) * (1.0 + mod_v[1]) + mod_v[0]
    flip = s == 0
    x1[0, 0] = jnp.where(flip, normed[HALF:], normed[:HALF]).astype(BF16)
    x1[1, 0] = jnp.where(flip, normed[:HALF], normed[HALF:]).astype(BF16)

    pl.semaphore_wait(barrier, len(peers))
    c_x = [spread_tokens(x1, o) for o in halves]

    c_st.wait()
    c_pt.wait()
    patch = patch_ref[0, 0]
    for k in range(3):
        low = st_v[k * TOK : (k + 1) * TOK, :]
        high = st_v[(k + 1) * TOK : (k + 2) * TOK, :]
        kv[k * TOK : (k + 1) * TOK, :] = jnp.where(patch <= k, high, low)

    c_wq.wait()
    for c in range(0, D, 128):
        wqt[c : c + 128, :] = wq_v[:, c : c + 128].T
    c_q = []
    for o in halves:
        arrive_all(c_x[o])
        c_q.append([])
        for a, b in QKV_CUTS:
            qkv = dot(x1[o].reshape(GROUPS * HALF, D), wqt[:, a:b]).astype(BF16)
            qs[o, :, :, a:b] = qkv.reshape(GROUPS, HALF, b - a)
            c_q[o] += [
                remote(qs.at[o, slot, :, a:b], qr.at[o, mine, :, a:b], dev)
                for slot, dev, _ in homeward[o]
            ]
            qr[o, mine, :, a:b] = qkv[0:HALF]

    c_wo.wait()
    for c in range(0, D, 128):
        wot[c : c + 128, :] = wo_v[:, c : c + 128].T
    c_fw.wait()
    channels = fw_v.shape[0]
    spots = HALF * channels
    fwt[...] = jnp.concatenate([fw_v[...]] * HALF, axis=0).T

    queries = []
    for o in halves:
        arrive_all(c_q[o])
        blocks = [qr[o, j].astype(F32) for j in range(GROUPS)]
        queries.append(jnp.concatenate([b[:, 0:BW] for b in blocks], axis=1))
        fresh = jnp.concatenate(
            [b[:, BW : 2 * BW] for b in blocks] + [b[:, 2 * BW :] for b in blocks], axis=1
        )
        kv[pl.ds(KEEP + rows[o], HALF), :] = fresh.astype(BF16)

    lane = lax.broadcasted_iota(jnp.int32, (TOK, WIN), 1)

    def heads_of(j):
        starts = [TOK * j + a * HEAD for a in range(HEADS // GROUPS)]
        return [(lane >= low) & (lane < low + HEAD) for low in starts]

    block = (HEADS // GROUPS) * TOK
    query = jnp.concatenate(queries, axis=0)
    for j in range(GROUPS):
        q = query[:, 256 * j : 256 * j + WIN]
        spread = jnp.concatenate([jnp.where(m, q, 0.0) for m in heads_of(j)], axis=0)
        sc[j * block : (j + 1) * block, :] = dot_t(
            spread.astype(BF16), kv[:, 256 * j : 256 * j + WIN]
        ) * HEAD ** (-0.5)
    scores = sc[...]
    raised = jnp.exp(scores - jnp.max(scores, axis=-1, keepdims=True))
    pb[...] = (raised / jnp.sum(raised, axis=-1, keepdims=True)).astype(BF16)
    wins = []
    for j in range(GROUPS):
        mixed = dot(pb[j * block : (j + 1) * block, :], kv[:, D + 256 * j : D + 256 * j + WIN])
        picked = jnp.zeros((TOK, WIN), F32)
        for a, m in enumerate(heads_of(j)):
            picked = jnp.where(m, mixed[a * TOK : (a + 1) * TOK], picked)
        wins.append(picked)
    cuts = [wins[0][:, 0:256]]
    for j in range(1, GROUPS):
        cuts.append(wins[j - 1][:, 256:WIN] + wins[j][:, 0:128])
        cuts.append(wins[j][:, 128:256])
    cuts.append(wins[GROUPS - 1][:, 256:WIN])
    whole = jnp.concatenate(cuts, axis=1).astype(BF16)
    c_m = []
    for o in halves:
        x2[o, 0] = whole[o * HALF : (o + 1) * HALF]
        c_m.append(spread_tokens(x2, o))

    c_p = []
    for o in halves:
        arrive_all(c_m[o])
        proj = dot(x2[o].reshape(GROUPS * HALF, D), wot[...]).astype(BF16)
        ps[o] = proj.reshape(GROUPS, HALF, BW)
        c_p.append([remote(ps.at[o, slot], pr.at[o, mine], dev) for slot, dev, _ in homeward[o]])
        pr[o, mine] = proj[0:HALF]

    c_u = []
    kept = []
    for o in halves:
        arrive_all(c_p[o])
        proj = jnp.concatenate([pr[o, j].astype(F32) for j in range(GROUPS)], axis=1)
        h1 = h_v[pl.ds(rows[o], HALF), :].astype(F32) + mod_v[2] * proj
        kept.append(h1)
        middle = layer_norm(h1) * (1.0 + mod_v[4]) + mod_v[3]
        x3[o, 0] = middle.astype(BF16)
        c_u.append(spread_tokens(x3, o))
        if o == 0:
            leave[...] = h1
            c_l = [remote(leave, arrive, other), remote(mod_v.at[5], gate, other)]

    fresh_out[...] = kv[KEEP:, :]
    c_wu.wait()
    c_wd.wait()
    early = list(sends)
    c_d = []
    for o in halves:
        arrive_all(c_u[o])
        inner_v[...] = jax.nn.gelu(
            dot(x3[o].reshape(GROUPS * HALF, D), wu_v[...]), approximate=True
        ).astype(BF16)
        own = []
        c_d.append([])
        for a, b in DOWN_CUTS:
            part = dot(inner_v[...], wd_v[:, a:b])
            own.append(part[0:HALF])
            parts[o, :, :, a:b] = part.astype(BF16).reshape(GROUPS, HALF, b - a)
            routes = crossing + [(0, other, GROUPS)] if o == 0 else homeward[o]
            into = rx if o == 0 else r4
            c_d[o] += [
                remote(parts.at[o, slot, :, a:b], into.at[i - 1, :, a:b], dev)
                for slot, dev, i in routes
            ]

    c_tm.wait()
    c_gp.wait()
    now = jnp.full((1, spots), time_ref[0], jnp.int32)
    before = jnp.full((1, spots), time_ref[0] - gap_ref[0], jnp.int32)
    now_bar = alpha_bar(now.astype(F32))
    prev_bar = alpha_bar(before.astype(F32))
    now_noise = jnp.sqrt(1.0 - now_bar)
    now_root = jnp.sqrt(now_bar)
    prev_noise = jnp.sqrt(1.0 - prev_bar)
    prev_root = jnp.sqrt(prev_bar)
    row = lax.broadcasted_iota(jnp.int32, (HALF, spots), 0)
    col = lax.broadcasted_iota(jnp.int32, (HALF, spots), 1)
    token = lax.div(col, channels) == row
    c_fm.wait()
    c_nz.wait()
    for c in early:
        c.wait_send()

    arrive_all(c_l)
    arrive_all(c_d[0])
    total = rx[0].astype(F32)
    for i in range(1, GROUPS):
        total = total + rx[i].astype(F32)
    out_across = arrive[...] + gate[...] * total
    for c in c_d[0]:
        c.wait_send()

    arrive_all(c_d[1])
    total = jnp.concatenate(own, axis=1)
    for i in range(GROUPS - 1):
        total = total + r4[i].astype(F32)
    out_here = kept[1] + mod_v[5] * total
    next_out[...] = jnp.where(flip, out_here, out_across).astype(BF16)
    final_rows = jnp.where(flip, out_across, out_here).astype(BF16).astype(F32)
    shifted = (layer_norm(final_rows) * (1.0 + fmod_v[1:2, :]) + fmod_v[0:1, :]).astype(BF16)
    each = dot(shifted, fwt[...])
    noise = jnp.sum(jnp.where(token, each, 0.0), axis=0, keepdims=True)
    clean = (noisy_v[...] - now_noise * noise) / now_root
    noise_out[...] = noise
    den_out[...] = prev_root * clean + prev_noise * noise

    for c in c_d[1]:
        c.wait_send()


def write_out(*refs):
    count = (len(refs) - 1) // 2
    sem = refs[-1]
    copies = [
        pltpu.make_async_copy(refs[i], refs[count + i], sem.at[i]) for i in range(count)
    ]
    for c in copies:
        c.start()
    for c in copies:
        c.wait()


def per_device(
    section_in,
    patch_index,
    stale_kv,
    modulation,
    final_mod,
    qkv_blocks,
    out_blocks,
    up_blocks,
    down_blocks,
    final_weight,
    noisy_latent,
    time_index,
    time_gap,
):
    any_spec = pl.BlockSpec(memory_space=pltpu.HBM)
    vmem = pl.BlockSpec(memory_space=pltpu.VMEM)
    spots = noisy_latent.shape[1]
    remote_count = 46
    outs = pl.pallas_call(
        kernel,
        name="relay_step",
        out_shape=(
            jax.ShapeDtypeStruct((TOK, 2 * D), BF16),
            jax.ShapeDtypeStruct((TOK // 2, D), BF16),
            jax.ShapeDtypeStruct((1, spots), F32),
            jax.ShapeDtypeStruct((1, spots), F32),
        ),
        in_specs=[any_spec] * 13,
        out_specs=(vmem,) * 4,
        scratch_shapes=[
            pltpu.SMEM((1, 1), jnp.int32),
            pltpu.SMEM((1,), jnp.int32),
            pltpu.SMEM((1,), jnp.int32),
            pltpu.VMEM((TOK, D), BF16),
            pltpu.VMEM((4 * TOK, 2 * D), BF16),
            pltpu.VMEM((6, 1, D), F32),
            pltpu.VMEM((2, D), F32),
            pltpu.VMEM((3 * BW, D), BF16),
            pltpu.VMEM((BW, D), BF16),
            pltpu.VMEM((D, D), BF16),
            pltpu.VMEM((D, D), BF16),
            pltpu.VMEM(final_weight.shape[::-1], BF16),
            pltpu.VMEM((1, spots), F32),
            pltpu.VMEM((D, 3 * BW), BF16),
            pltpu.VMEM((D, BW), BF16),
            pltpu.VMEM((D, spots), BF16),
            pltpu.VMEM((HEADS * TOK, KEEP + TOK), F32),
            pltpu.VMEM((HEADS * TOK, KEEP + TOK), BF16),
            pltpu.VMEM((2, GROUPS, HALF, D), BF16),
            pltpu.VMEM((2, GROUPS, HALF, 3 * BW), BF16),
            pltpu.VMEM((2, GROUPS, HALF, 3 * BW), BF16),
            pltpu.VMEM((KEEP + TOK, 2 * D), BF16),
            pltpu.VMEM((2, GROUPS, HALF, D), BF16),
            pltpu.VMEM((2, GROUPS, HALF, BW), BF16),
            pltpu.VMEM((2, GROUPS, HALF, BW), BF16),
            pltpu.VMEM((2, GROUPS, HALF, D), BF16),
            pltpu.VMEM((GROUPS * HALF, D), BF16),
            pltpu.VMEM((2, GROUPS, HALF, D), BF16),
            pltpu.VMEM((GROUPS - 1, HALF, D), BF16),
            pltpu.VMEM((GROUPS, HALF, D), BF16),
            pltpu.VMEM((HALF, D), F32),
            pltpu.VMEM((HALF, D), F32),
            pltpu.VMEM((1, D), F32),
            pltpu.SemaphoreType.DMA((13,)),
            pltpu.SemaphoreType.DMA((remote_count,)),
            pltpu.SemaphoreType.DMA((remote_count,)),
        ],
        compiler_params=pltpu.CompilerParams(
            collective_id=0, has_side_effects=True, vmem_limit_bytes=48 * 1024 * 1024
        ),
    )(
        patch_index,
        time_index,
        time_gap,
        *(pltpu.with_memory_space_constraint(a, pltpu.HBM) for a in (        section_in[0, 0],
        stale_kv[0, 0],
        modulation[0, 0][:, None, :],
        final_mod[0],
        qkv_blocks[0, 0].T,
        out_blocks[0, 0].T,
        up_blocks[0, 0],
        down_blocks[0, 0],
        final_weight.T,
        noisy_latent,))
    )
    fresh, next_rows, noise_pred, denoised = pl.pallas_call(
        write_out,
        name="write_out",
        out_shape=tuple(jax.ShapeDtypeStruct(o.shape, o.dtype) for o in outs),
        in_specs=(vmem,) * 4,
        out_specs=(any_spec,) * 4,
        scratch_shapes=[pltpu.SemaphoreType.DMA((4,))],
    )(*(pltpu.with_memory_space_constraint(o, pltpu.VMEM) for o in outs))
    return (fresh[None, None], next_rows[None], noise_pred, denoised)


def solution(mesh):
    placed = (
        P("section", "req", None, None),
        P("section", "req"),
        P("section", "req", None, None),
        P("section", "req", None, None),
        P("req", None, None),
        P("section", "req", None, None),
        P("section", "req", None, None),
        P("section", "req", None, None),
        P("section", "req", None, None),
        P(),
        P("req", "section"),
        P("req"),
        P("req"),
    )
    return jax.shard_map(
        per_device,
        mesh=mesh,
        in_specs=placed,
        out_specs=(
            P("section", "req", None, None),
            P("req", "section", None),
            P("req", "section"),
            P("req", "section"),
        ),
        check_vma=False,
    )
```
